32 devices in a mesh: ctx: 16 (over z, y, core), ch: 2 (over x).
Axes of the slice: x: 2, y: 2, z: 4, core: 2. Of those that a mesh axis runs over, the one named last changes fastest.
Arguments:
- query_proj: bfloat16 [2048, 8192], P('ctx', 'ch'), may hold values from -31 to 31
- key_proj: bfloat16 [2048, 8192], P('ctx', 'ch'), may hold values from -6 to 6
- value_proj: bfloat16 [2048, 8192], P('ctx', 'ch'), may hold values from -6 to 6
- key_taps: bfloat16 [512, 3], P('ch'), may hold values from -3.5 to 3.5
- value_taps: bfloat16 [512, 3], P('ch'), may hold values from -3.5 to 3.5
- residues: float32 [512, 16], P('ch'), may hold values from -0.06 to 0.06
- decay_rates: float32 [512, 16], P('ch'), may hold values from 5e-06 to 0.05
- skip_weight: float32 [8192], P('ch'), may hold values from 0.5 to 1.5
- norm_gain: float32 [8192], P('ch'), may hold values from 0.5 to 1.5
- out_grad: bfloat16 [2048, 8192], P('ctx', 'ch'), may hold values from -6 to 6
Outputs:
- mixed_out: bfloat16 [2048, 8192], P('ctx', 'ch')
- query_grad: bfloat16 [2048, 8192], P('ctx', 'ch')
- key_grad: bfloat16 [2048, 8192], P('ctx', 'ch')
- value_grad: bfloat16 [2048, 8192], P('ctx', 'ch')
- key_taps_grad: float32 [512, 3], P('ch')
- value_taps_grad: float32 [512, 3], P('ch')
- skip_grad: float32 [8192], P('ch')
- gain_grad: float32 [8192], P('ch')
The draws below stay inside these ranges and needn't reach their ends.
All inputs are finite; a program needn't handle non-finite values.
Results may differ from the reference program's by a relative error of at most 0.006.
Values may be sent and summed in bfloat16 or wider, within the bound.
A program may use at most 128 MiB of HBM per device.

```python
import jax
import jax.numpy as jnp
from jax import lax

D = 8192
ORDER = 3
MODES = 16
TOKENS = 2048
GROUPS = 512


def draw_query_proj(key, part):
    column = jnp.arange(D).astype(jnp.float32) / D
    rising = jnp.exp(jnp.log(3.0) * column)
    values = jnp.clip(jax.random.normal(key, (TOKENS, D), jnp.float32), -6.0, 6.0) * rising
    return values.astype(jnp.bfloat16)


def mode_kinds(key):
    bits = jax.random.randint(jax.random.fold_in(key, 7001), (GROUPS, MODES), 0, 2)
    return bits == 1


def draw_decay_rates(key, part):
    quick = mode_kinds(key)
    key_fast, key_slow = jax.random.split(jax.random.fold_in(key, 7002))
    fast_rates = jnp.exp(jax.random.uniform(key_fast, (GROUPS, MODES), jnp.float32, jnp.log(0.01), jnp.log(0.05)))
    slow_rates = jnp.exp(jax.random.uniform(key_slow, (GROUPS, MODES), jnp.float32, jnp.log(5e-06), jnp.log(0.0002)))
    rates = jnp.where(quick, fast_rates, slow_rates)
    return jnp.clip(rates, 5e-06, 0.05).astype(jnp.float32)


def draw_residues(key, part):
    quick = mode_kinds(key)
    key_sign, key_fast, key_slow = jax.random.split(jax.random.fold_in(key, 7003), 3)
    signs = (2 * jax.random.randint(key_sign, (GROUPS, 1), 0, 2) - 1).astype(jnp.float32)
    fast_size = jax.random.uniform(key_fast, (GROUPS, MODES), jnp.float32, 0.03, 0.06)
    slow_size = jax.random.uniform(key_slow, (GROUPS, MODES), jnp.float32, 0.002, 0.008)
    values = signs * jnp.where(quick, fast_size, slow_size)
    return jnp.clip(values, -0.06, 0.06).astype(jnp.float32)


def levels(key, extent, pieces, smallest, high):
    factor_of, own = 1.0, jax.random.fold_in(key, 6)
    for position, parts in pieces:
        heights = jnp.exp(jax.random.uniform(jax.random.fold_in(own, position), (parts,), jnp.float32, smallest / len(pieces), high / len(pieces)))
        factor_of = factor_of * jnp.repeat(heights, extent[position] // parts).reshape([-1 if axis == position else 1 for axis in range(len(extent))])
    return factor_of


def centred(stream_key, dims, scale, limit, pieces=(), dtype=jnp.bfloat16):
    entries = jax.random.normal(stream_key, dims, jnp.float32) * scale
    if len(pieces) > 0:
        entries = levels(stream_key, dims, pieces, -0.22, 0.18) * entries
    return jnp.clip(entries, min=-limit, max=limit).astype(dtype)


def setup_inputs(seed: int = 0) -> dict:
    key_of = jax.random.split(jax.random.key(seed), 11)
    return {
        "query_proj": draw_query_proj(jax.random.fold_in(key_of[10], 71), 0),
        "key_proj": centred(key_of[1], (TOKENS, D), 1.0, 6.0, ((0, 16), (1, 2))),
        "value_proj": centred(key_of[2], (TOKENS, D), 1.0, 6.0, ((0, 16), (1, 2))),
        "key_taps": centred(key_of[3], (GROUPS, ORDER), ORDER ** -0.5, 3.5, ((0, 2),)),
        "value_taps": centred(key_of[4], (GROUPS, ORDER), ORDER ** -0.5, 3.5, ((0, 2),)),
        "residues": draw_residues(jax.random.fold_in(key_of[10], 71), 0),
        "decay_rates": draw_decay_rates(jax.random.fold_in(key_of[10], 71), 0),
        "skip_weight": jnp.clip(0.5 + 1.0 * jax.random.uniform(key_of[7], (D,), jnp.float32) ** levels(key_of[7], (D,), ((0, 2),), -0.2, 0.2), 0.5, 1.5),
        "norm_gain": jnp.clip(1.0 + 0.1 * jax.random.normal(key_of[8], (D,), jnp.float32), 0.5, 1.5),
        "out_grad": centred(key_of[9], (TOKENS, D), 1.0, 6.0, ((0, 16), (1, 2))),
    }


EPSILON = 1e-06

def decay_filter(residues, decay_rates, length):
    lagged = jnp.arange(length).astype(jnp.float32)
    return lax.optimization_barrier(jnp.sum(residues[:, :, None] * jnp.exp(-decay_rates[:, :, None] * lagged[None, None, :]), axis=1))

def spread_groups(table, width):
    return jnp.repeat(table, width // table.shape[0], axis=0)

def short_conv(signal, taps):
    tap_count = taps.shape[1]
    length, width = signal.shape
    padded = jnp.concatenate([jnp.zeros((tap_count - 1, width), jnp.float32), signal.astype(jnp.float32)], 0)
    spread = spread_groups(taps.astype(jnp.float32), width)

    def add_tap(offset, accum):
        begin = (tap_count - 1 - offset).astype(jnp.int32)
        window = lax.dynamic_slice_in_dim(padded, begin, length, 0)
        column = lax.dynamic_index_in_dim(spread, offset.astype(jnp.int32), 1, keepdims=False)
        return accum + window * column[None, :]
    return lax.fori_loop(0, tap_count, add_tap, jnp.zeros((length, width), jnp.float32))

def short_adjoint(grad_rows, taps):
    tap_count = taps.shape[1]
    length, width = grad_rows.shape
    padded = jnp.concatenate([grad_rows.astype(jnp.float32), jnp.zeros((tap_count - 1, width), jnp.float32)], 0)
    spread = spread_groups(taps.astype(jnp.float32), width)

    def add_tap(offset, accum):
        window = lax.dynamic_slice_in_dim(padded, offset.astype(jnp.int32), length, 0)
        column = lax.dynamic_index_in_dim(spread, offset.astype(jnp.int32), 1, keepdims=False)
        return accum + window * column[None, :]
    return lax.fori_loop(0, tap_count, add_tap, jnp.zeros((length, width), jnp.float32))

def taps_gradient(grad_rows, signal, groups, tap_count):
    length, width = signal.shape
    padded = jnp.concatenate([jnp.zeros((tap_count - 1, width), jnp.float32), signal.astype(jnp.float32)], 0)
    grad_wide = grad_rows.astype(jnp.float32)

    def one_tap(offset):
        begin = (tap_count - 1 - offset).astype(jnp.int32)
        window = lax.dynamic_slice_in_dim(padded, begin, length, 0)
        per_channel = lax.optimization_barrier(jnp.sum(grad_wide * window, axis=0))
        return lax.optimization_barrier(jnp.sum(per_channel.reshape(groups, width // groups), axis=1))
    return lax.map(one_tap, jnp.arange(tap_count).astype(jnp.int32)).T

def causal_long(signal, filt):
    length = signal.shape[0]
    spectrum = jnp.fft.rfft(signal, n=2 * length, axis=0)
    kernel = jnp.fft.rfft(filt, n=2 * length, axis=1)
    kernel = spread_groups(kernel, signal.shape[1]).T
    return jnp.fft.irfft(spectrum * kernel, n=2 * length, axis=0)[:length]

def reference(query_proj, key_proj, value_proj, key_taps, value_taps, residues, decay_rates, skip_weight, norm_gain, out_grad):
    groups, tap_count = key_taps.shape
    width = key_proj.shape[1]
    length = key_proj.shape[0]
    key_mixed = short_conv(key_proj, key_taps)
    value_mixed = short_conv(value_proj, value_taps)
    product = (key_mixed * value_mixed).astype(jnp.bfloat16)
    filt = decay_filter(residues, decay_rates, length)
    product_wide = product.astype(jnp.float32)
    mixed = causal_long(product_wide, filt) + skip_weight[None, :] * product_wide
    query_wide = query_proj.astype(jnp.float32)
    gated = query_wide * mixed
    squares = lax.optimization_barrier(jnp.sum(gated * gated, axis=1))
    scaled = lax.rsqrt(squares / width + EPSILON)[:, None]
    mixed_out = (gated * scaled * norm_gain).astype(jnp.bfloat16)
    grad_wide = out_grad.astype(jnp.float32)
    projected = lax.optimization_barrier(jnp.sum(gated * norm_gain * grad_wide, axis=1))
    gated_grad = scaled * norm_gain * grad_wide - gated * (scaled * scaled * scaled * projected[:, None] / width)
    gain_grad = lax.optimization_barrier(jnp.sum(grad_wide * gated * scaled, axis=0))
    query_grad = (gated_grad * mixed).astype(jnp.bfloat16)
    mixed_grad = (gated_grad * query_wide).astype(jnp.bfloat16)
    mixed_grad_wide = mixed_grad.astype(jnp.float32)
    backward_long = jnp.flip(causal_long(jnp.flip(mixed_grad_wide, 0), filt), 0)
    product_grad = backward_long + skip_weight[None, :] * mixed_grad_wide
    skip_grad = lax.optimization_barrier(jnp.sum(mixed_grad_wide * product_wide, axis=0))
    key_mixed_grad = (product_grad * value_mixed).astype(jnp.bfloat16)
    value_mixed_grad = (product_grad * key_mixed).astype(jnp.bfloat16)
    key_grad = short_adjoint(key_mixed_grad, key_taps).astype(jnp.bfloat16)
    value_grad = short_adjoint(value_mixed_grad, value_taps).astype(jnp.bfloat16)
    key_taps_grad = taps_gradient(key_mixed_grad, key_proj, groups, tap_count)
    value_taps_grad = taps_gradient(value_mixed_grad, value_proj, groups, tap_count)
    return (mixed_out, query_grad, key_grad, value_grad, key_taps_grad, value_taps_grad, skip_grad, gain_grad)
```

```python
import functools

import jax
import jax.numpy as jnp
from jax import lax
from jax.experimental import pallas as pl
from jax.experimental.pallas import tpu as pltpu
from jax.sharding import PartitionSpec as P

EPSILON = 1e-06
TILE = 256
LANES = 128
CHUNK = 32
F32, BF16 = jnp.float32, jnp.bfloat16


def halves(wide):
    high = wide.astype(BF16)
    return high, (wide - high.astype(F32)).astype(BF16)


def body(
    n, n_ch, slices, width_all, group_size,
    q_hbm, k_hbm, v_hbm, kt_ref, vt_ref, res_ref, rates_ref, skip_ref, gain_ref, og_hbm,
    out_ref, qg_ref, kg_ref, vg_ref, ktg_ref, vtg_ref, skg_ref, gng_ref,
    q_ref, k_ref, v_ref, og_ref, io_sem, small, rate_line,
    tail_out, tail_in, head_out, head_in, before, last, taps,
    lag_up, lag_down, up_turned, down_turned, filt, turned, mask_half,
    prod, kmix, vmix, mixed, mgrad, kmg, vmg, tap_rows,
    own, gathered, prefix, incoming,
    own_b, gathered_b, suffix, incoming_b,
    part, parts, total, mine, others,
    row_acc, row_out, row_in,
    tail_sem, head_sem, send_sem, recv_sem, ch_send, ch_recv,
):
    me = lax.axis_index("ctx")
    me_ch = lax.axis_index("ch")
    rows = q_ref.shape[0]
    groups = rates_ref.shape[1]
    groups_tile = TILE // group_size
    groups_lanes = LANES // group_size
    load_k, load_v, load_q, load_og = (
        pltpu.make_async_copy(src, dst, io_sem.at[place])
        for place, (src, dst) in enumerate(
            ((k_hbm, k_ref), (v_hbm, v_ref), (q_hbm, q_ref), (og_hbm, og_ref))
        )
    )

    def to_ctx(src, dst, s_sem, r_sem, peer):
        return pltpu.make_async_remote_copy(
            src_ref=src, dst_ref=dst, send_sem=s_sem, recv_sem=r_sem,
            device_id={"ctx": peer}, device_id_type=pl.DeviceIdType.MESH,
        )

    def columns(j):
        return pl.ds(pl.multiple_of(j * TILE, TILE), TILE)

    def group_rows(j):
        return pl.ds(pl.multiple_of(j * groups_tile, groups_tile), groups_tile)

    barrier = pltpu.get_barrier_semaphore()

    @pl.loop(1, n)
    def _(i):
        pl.semaphore_signal(
            barrier, inc=1, device_id={"ctx": lax.rem(me + i, n)},
            device_id_type=pl.DeviceIdType.MESH,
        )

    for i in range(1, n_ch):
        pl.semaphore_signal(
            barrier, inc=1, device_id={"ch": lax.rem(me_ch + i, n_ch)},
            device_id_type=pl.DeviceIdType.MESH,
        )
    for load in (load_k, load_v, load_q, load_og):
        load.start()

    lane = lax.broadcasted_iota(jnp.int32, (group_size, LANES), 1)
    sub = lax.broadcasted_iota(jnp.int32, (group_size, LANES), 0)
    lane_wide = lane.astype(F32)
    backwards = LANES - 1 - lane
    own_lane = sub == lax.rem(lane, group_size)
    small[...] = jnp.zeros(small.shape, F32)
    small[0:16, 0:groups] = rates_ref[...]
    small[16:32, 0:groups] = res_ref[...]
    small[32:35, 0:groups] = kt_ref[...].astype(F32)
    small[35:38, 0:groups] = vt_ref[...].astype(F32)

    def source_of(first):
        start = (first // LANES) * LANES
        return pl.ds(pl.multiple_of(start, LANES), LANES), first - start

    def pick(table, index):
        return jnp.take_along_axis(table, index, axis=1)

    def of_channels(kind, block):
        source, first = source_of(block * groups_lanes)
        return pick(small[kind, source], first + lane // group_size)

    @pl.loop(0, slices * TILE // LANES)
    def _(block):
        cols = pl.ds(pl.multiple_of(block * LANES, LANES), LANES)
        source, first = source_of(block * groups_lanes)
        chosen = first + lane // group_size
        rates = pick(small[0:16, source], chosen)
        rate_line[0:1, cols] = jnp.sum(jnp.where(own_lane, rates, 0.0), axis=0, keepdims=True)
        taps[0:8, cols] = pick(small[32:40, source], chosen[0:8])

    block_mask = (
        lax.broadcasted_iota(jnp.int32, (TILE, TILE), 0) // group_size
        == lax.broadcasted_iota(jnp.int32, (TILE, TILE), 1) // group_size
    )
    mask_half[...] = block_mask.astype(F32).astype(BF16)

    load_k.wait()
    load_v.wait()
    tail_out[0:2] = k_ref[rows - 16 : rows].astype(F32)[14:16]
    tail_out[2:4] = v_ref[rows - 16 : rows].astype(F32)[14:16]
    tails = to_ctx(tail_out, tail_in, tail_sem.at[0], tail_sem.at[1], lax.rem(me + 1, n))
    heads = to_ctx(head_out, head_in, head_sem.at[0], head_sem.at[1], lax.rem(me + n - 1, n))
    pl.semaphore_wait(barrier, n - 1 + n_ch - 1)

    @pl.when(me < n - 1)
    def _():
        tails.start()

    @pl.when(me == 0)
    def _():
        tail_in[...] = jnp.zeros(tail_in.shape, F32)

    row8 = lax.broadcasted_iota(jnp.int32, (8, TILE), 0).astype(F32)
    row_steps = lax.broadcasted_iota(jnp.int32, (rows // 8, TILE), 0).astype(F32) * 8.0

    @pl.loop(0, slices)
    def _(j):
        cols = columns(j)
        rate = rate_line[0:1, cols]
        steps = jnp.exp(-rate * row_steps)
        up8 = jnp.exp(-rate * row8)
        down8 = jnp.exp(-rate * (7.0 - row8))
        count = rows // 8
        for table, piece, order in (
            (lag_up, up8, range(count)), (lag_down, down8, reversed(range(count)))
        ):
            high, low = halves(jnp.concatenate([piece * steps[a : a + 1] for a in order], axis=0))
            table[0:rows, cols] = high
            table[rows : 2 * rows, cols] = low
        source, first = source_of(j * groups_tile)
        rates, residues = small[0:16, source], small[16:32, source]
        lines = []
        for g in range(groups_tile):
            index = jnp.broadcast_to(first + g, (group_size, LANES))
            fade = jnp.exp(-pick(rates, index) * lane_wide)
            lines.append(jnp.sum(pick(residues, index) * fade, axis=0, keepdims=True))
            at = pl.ds(pl.multiple_of(j * TILE + g * group_size, group_size), group_size)
            for table, wide in ((up_turned, fade), (down_turned, pick(fade, backwards))):
                high, low = halves(wide)
                table[at, 0:LANES] = high
                table[at, LANES : 2 * LANES] = low
        lines = jnp.concatenate(lines, axis=0)
        filt[group_rows(j), :] = lines
        turned[group_rows(j), :] = pick(lines, backwards)

    lane_group = lax.broadcasted_iota(jnp.int32, (CHUNK, TILE), 1) // group_size
    tri_row = lax.broadcasted_iota(jnp.int32, (rows, rows), 0)
    tri_col = lax.broadcasted_iota(jnp.int32, (rows, rows), 1)

    @pl.when(me > 0)
    def _():
        tails.wait_recv()

    before[0, 14:16] = tail_in[0:2]
    before[1, 14:16] = tail_in[2:4]

    def delayed(ref, cols, which, r):
        if r == 0:
            wide = jnp.concatenate([before[which, :, cols], ref[0:CHUNK, cols].astype(F32)], axis=0)
        else:
            wide = ref[r - 16 : r + CHUNK, cols].astype(F32)
        return wide[16 : 16 + CHUNK], wide[15 : 15 + CHUNK], wide[14 : 14 + CHUNK]

    def mix(parts_of, cols, base):
        zero, one, two = parts_of
        return (
            zero * taps[base : base + 1, cols]
            + one * taps[base + 1 : base + 2, cols]
            + two * taps[base + 2 : base + 3, cols]
        )

    def folded(x):
        return jnp.sum(x.reshape(x.shape[0] // 8, 8, TILE), axis=0)

    def modal(table, j, signal):
        full = jnp.dot(
            table[columns(j), :], jnp.concatenate([signal, signal], axis=0),
            preferred_element_type=F32,
        )
        kept = jnp.where(block_mask, full, 0.0)
        return jnp.sum(kept.reshape(groups_tile, group_size, TILE), axis=0).astype(BF16)

    def spread(table, cols, state):
        big = jnp.concatenate([state] * groups_tile, axis=0) * mask_half[...]
        return jnp.dot(
            jnp.concatenate([table[0:rows, cols], table[rows : 2 * rows, cols]], axis=1),
            jnp.concatenate([big, big], axis=0),
            preferred_element_type=F32,
        )

    def toeplitz(table, shift, j, ref, cols, keep):
        lines = table[group_rows(j), :]
        lhs, rhs = [], []
        for g in range(groups_tile):
            spread_line = jnp.broadcast_to(lines[g : g + 1, :], (rows, rows))
            turned_line = pltpu.roll(spread_line, shift, 1, stride=1, stride_axis=0)
            lhs.append(jnp.where(keep, turned_line, 0.0).astype(BF16))
            for r in range(0, rows, CHUNK):
                wide = ref[r : r + CHUNK, cols].astype(F32)
                rhs.append(jnp.where(lane_group == g, wide, 0.0).astype(BF16))
        return jnp.dot(
            jnp.concatenate(lhs, axis=1), jnp.concatenate(rhs, axis=0),
            preferred_element_type=F32,
        )

    def scatter(phase, source, target, j):
        copy = to_ctx(
            source.at[j], target.at[me], send_sem.at[phase], recv_sem.at[phase, me], j
        )

        @pl.when(j != me)
        def _():
            copy.start()

        @pl.when(j == me)
        def _():
            target[me] = source[j]

    def arrive(phase, source, target, i):
        @pl.when(i != me)
        def _():
            to_ctx(
                source.at[0], target.at[i], send_sem.at[phase], recv_sem.at[phase, i], i
            ).wait_recv()

    def sent(phase, source, count):
        if count:
            whole = source.at[pl.ds(0, count)]
            pltpu.make_async_copy(whole, whole, send_sem.at[phase]).wait()

    def sent_slices(phase, source):
        if n == slices:
            sent(phase, source, slices - 1)
        else:
            @pl.when(me < slices)
            def _():
                sent(phase, source, slices - 1)

            @pl.when(me >= slices)
            def _():
                sent(phase, source, slices)

    def of_owner():
        rate, residue = (
            jnp.concatenate([of_channels(kind, 2 * me), of_channels(kind, 2 * me + 1)], axis=1)
            for kind in (slice(0, 16), slice(16, 32))
        )
        return jnp.exp(-rate * float(rows)), residue * jnp.exp(-rate)

    @pl.loop(0, slices)
    def _(i):
        j = lax.rem(me + i, slices)
        cols = columns(j)
        for r in range(0, rows, CHUNK):
            part_rows = slice(r, r + CHUNK)
            key = mix(delayed(k_ref, cols, 0, r), cols, 0)
            value = mix(delayed(v_ref, cols, 1, r), cols, 3)
            kmix[part_rows, cols] = key
            vmix[part_rows, cols] = value
            prod[part_rows, cols] = (key * value).astype(BF16)
        own[j] = modal(down_turned, j, prod[:, cols])
        scatter(0, own, gathered, j)

    def long_forward(j):
        cols = columns(j)
        mixed[:, cols] = toeplitz(turned, 1, j, prod, cols, tri_row >= tri_col)

    early = slices // 2

    @pl.loop(0, early)
    def _(j):
        long_forward(j)

    @pl.when(me < slices)
    def _():
        fall, scale = of_owner()

        def step(i, carry):
            prefix[i] = (carry * scale).astype(BF16)
            scatter(1, prefix, incoming, i)
            arrive(0, own, gathered, i)
            return fall * carry + gathered[i].astype(F32)

        lax.fori_loop(0, n, step, jnp.zeros((group_size, TILE), F32))

    @pl.loop(early, slices)
    def _(j):
        long_forward(j)

    row_acc[...] = jnp.zeros(row_acc.shape, F32)
    load_q.wait()
    load_og.wait()

    @pl.loop(0, slices)
    def _(i):
        j = lax.rem(me + i, slices)
        cols = columns(j)
        arrive(1, prefix, incoming, j)
        mixed[:, cols] += spread(lag_up, cols, incoming[j])
        for r in range(0, rows, CHUNK):
            part_rows = slice(r, r + CHUNK)
            full = mixed[part_rows, cols] + skip_ref[0:1, cols] * prod[part_rows, cols].astype(F32)
            mixed[part_rows, cols] = full
            gated = q_ref[part_rows, cols].astype(F32) * full
            squares = gated * gated
            along = gated * gain_ref[0:1, cols] * og_ref[part_rows, cols].astype(F32)
            row_acc[0, part_rows] += squares[:, :128] + squares[:, 128:]
            row_acc[1, part_rows] += along[:, :128] + along[:, 128:]

    both = row_acc[...].reshape(2 * rows, LANES)
    high, low = halves(both)
    lowest = (both - high.astype(F32) - low.astype(F32)).astype(BF16)
    row_out[...] = lax.dot_general(
        jnp.ones((16, 3 * LANES), BF16), jnp.concatenate([high, low, lowest], axis=1),
        (((1,), (1,)), ((), ())), preferred_element_type=F32,
    )[0:8]

    def to_ch(i):
        return pltpu.make_async_remote_copy(
            src_ref=row_out, dst_ref=row_in.at[i - 1], send_sem=ch_send.at[i - 1],
            recv_sem=ch_recv.at[i - 1], device_id={"ch": lax.rem(me_ch + i, n_ch)},
            device_id_type=pl.DeviceIdType.MESH,
        )

    for i in range(1, n_ch):
        to_ch(i).start()
    summed = row_out[...]
    for i in range(1, n_ch):
        to_ch(i).wait_recv()
        summed = summed + row_in[i - 1]
    squares, along = summed[:, 0:rows], summed[:, rows : 2 * rows]
    scaled = lax.rsqrt(squares / width_all + EPSILON)
    pull = scaled * scaled * scaled * along / width_all
    row_acc[0] = jnp.broadcast_to(scaled[0:1], (rows, rows)).T
    row_acc[1] = jnp.broadcast_to(pull[0:1], (rows, rows)).T

    @pl.loop(0, slices)
    def _(i):
        j = lax.rem(me + i, slices)
        cols = columns(j)
        gain = gain_ref[0:1, cols]
        skip_sum = gain_sum = jnp.zeros((8, TILE), F32)
        for r in range(0, rows, CHUNK):
            part_rows = slice(r, r + CHUNK)
            scaled = jnp.concatenate([row_acc[0, part_rows]] * 2, axis=1)
            pull = jnp.concatenate([row_acc[1, part_rows]] * 2, axis=1)
            query = q_ref[part_rows, cols].astype(F32)
            grad = og_ref[part_rows, cols].astype(F32)
            full = mixed[part_rows, cols]
            gated = query * full
            normed = gated * scaled
            out_ref[part_rows, cols] = (normed * gain).astype(BF16)
            gated_grad = scaled * gain * grad - gated * pull
            qg_ref[part_rows, cols] = (gated_grad * full).astype(BF16)
            mixed_grad = (gated_grad * query).astype(BF16)
            mgrad[part_rows, cols] = mixed_grad
            skip_sum += folded(mixed_grad.astype(F32) * prod[part_rows, cols].astype(F32))
            gain_sum += folded(grad * normed)
        own_b[j] = modal(up_turned, j, mgrad[:, cols])
        scatter(2, own_b, gathered_b, j)
        part[j, 0:1, :] = jnp.sum(skip_sum, axis=0, keepdims=True)
        part[j, 1:2, :] = jnp.sum(gain_sum, axis=0, keepdims=True)
        scatter(4, part, parts, j)

    def long_backward(j):
        cols = columns(j)
        mixed[:, cols] = toeplitz(filt, 0, j, mgrad, cols, tri_row <= tri_col)

    @pl.loop(0, early)
    def _(j):
        long_backward(j)

    @pl.when(me < slices)
    def _():
        fall, scale = of_owner()

        def step(i, carry):
            place = n - 1 - i
            suffix[place] = (carry * scale).astype(BF16)
            scatter(3, suffix, incoming_b, place)
            arrive(2, own_b, gathered_b, place)
            return fall * carry + gathered_b[place].astype(F32)

        lax.fori_loop(0, n, step, jnp.zeros((group_size, TILE), F32))

        def add(i, carry):
            arrive(4, part, parts, i)
            return carry + parts[i]

        total[me] = lax.fori_loop(0, n, add, jnp.zeros((2, TILE), F32))

        @pl.loop(0, n)
        def _(i):
            @pl.when(i != me)
            def _():
                to_ctx(
                    total.at[me], total.at[me], send_sem.at[5], recv_sem.at[5, me], i
                ).start()

    @pl.loop(early, slices)
    def _(j):
        long_backward(j)

    @pl.loop(0, slices)
    def _(i):
        j = lax.rem(me + i, slices)
        cols = columns(j)
        arrive(3, suffix, incoming_b, j)
        mixed[:, cols] += spread(lag_down, cols, incoming_b[j])
        sums = [jnp.zeros((8, TILE), F32)] * 6
        later = [jnp.zeros((8, TILE), F32)] * 2
        for r in reversed(range(0, rows, CHUNK)):
            part_rows = slice(r, r + CHUNK)
            pgrad = (
                mixed[part_rows, cols] + skip_ref[0:1, cols] * mgrad[part_rows, cols].astype(F32)
            )
            for which, (other, signal, target) in enumerate(
                ((vmix, k_ref, kmg), (kmix, v_ref, vmg))
            ):
                half = (pgrad * other[part_rows, cols]).astype(BF16)
                target[part_rows, cols] = half
                zero = half.astype(F32)
                wide = jnp.concatenate([zero, later[which]], axis=0)
                shifted = (zero, wide[1 : 1 + CHUNK], wide[2 : 2 + CHUNK])
                later[which] = zero[0:8]
                inside = signal[part_rows, cols].astype(F32)
                for offset in range(3):
                    place = 3 * which + offset
                    sums[place] = sums[place] + folded(shifted[offset] * inside)
        tap_sums = []
        for which in range(2):
            first, second = later[which][0:1], later[which][1:2]
            head_out[2 * which : 2 * which + 2, cols] = later[which][0:2]
            older = tail_in[2 * which : 2 * which + 1, cols]
            newer = tail_in[2 * which + 1 : 2 * which + 2, cols]
            edges = (0.0, first * newer, first * older + second * newer)
            for offset in range(3):
                tap_sums.append(
                    jnp.sum(sums[3 * which + offset], axis=0, keepdims=True) + edges[offset]
                )
        tap_sums = jnp.concatenate(tap_sums + [jnp.zeros((2, TILE), F32)], axis=0)
        high = tap_sums.astype(BF16).astype(F32)
        at = pl.ds(pl.multiple_of(j * 16, 16), 16)
        tap_rows[at, :] = jnp.concatenate([high, tap_sums - high], axis=0).astype(BF16)

    @pl.when(me > 0)
    def _():
        heads.start()

    @pl.when(me == n - 1)
    def _():
        head_in[...] = jnp.zeros(head_in.shape, F32)

    member = (
        lax.broadcasted_iota(jnp.int32, (TILE, LANES), 0) // group_size
        == lax.broadcasted_iota(jnp.int32, (TILE, LANES), 1)
    ).astype(F32).astype(BF16)
    grouped = jnp.dot(tap_rows[...], member, preferred_element_type=F32)
    fields = [jnp.zeros((8, LANES), F32)] * (mine.shape[1] // LANES)
    for j in range(slices):
        here = grouped[16 * j : 16 * j + 8] + grouped[16 * j + 8 : 16 * j + 16]
        field, start = divmod(j * groups_tile, LANES)
        fields[field] = fields[field] + (pltpu.roll(here, start, 1) if start else here)
    for field, value in enumerate(fields):
        mine[:, field * LANES : (field + 1) * LANES] = value

    @pl.loop(1, n)
    def _(i):
        to_ctx(
            mine, others.at[me], send_sem.at[6], recv_sem.at[6, me], lax.rem(me + i, n)
        ).start()

    def adjoint(j, r):
        cols = columns(j)
        for which, (source, target) in enumerate(((kmg, kg_ref), (vmg, vg_ref))):
            if r + CHUNK < rows:
                wide = source[r : r + CHUNK + 16, cols].astype(F32)
            else:
                wide = jnp.concatenate(
                    [source[r : r + CHUNK, cols].astype(F32), last[which, :, cols]], axis=0
                )
            shifted = (wide[0:CHUNK], wide[1 : 1 + CHUNK], wide[2 : 2 + CHUNK])
            target[r : r + CHUNK, cols] = mix(shifted, cols, 3 * which).astype(BF16)

    @pl.loop(0, slices)
    def _(j):
        for r in range(0, rows - CHUNK, CHUNK):
            adjoint(j, r)

    @pl.when(me < n - 1)
    def _():
        heads.wait_recv()

    last[0, 0:2] = head_in[0:2]
    last[1, 0:2] = head_in[2:4]

    @pl.loop(0, slices)
    def _(j):
        adjoint(j, rows - CHUNK)

        @pl.when(j != me)
        def _():
            to_ctx(
                total.at[j], total.at[j], send_sem.at[5], recv_sem.at[5, j], j
            ).wait_recv()

        cols = columns(j)
        here = total[j]
        skg_ref[0:1, cols] = here[0:1]
        gng_ref[0:1, cols] = here[1:2]

    others[me] = mine[...]

    def gather(i, carry):
        arrive(6, others, others, i)
        return carry + others[i]

    summed = lax.fori_loop(0, n, gather, jnp.zeros(mine.shape, F32))[:, 0:groups]
    ktg_ref[...] = summed[0:3]
    vtg_ref[...] = summed[3:6]

    @pl.when(me < n - 1)
    def _():
        tails.wait_send()

    @pl.when(me > 0)
    def _():
        heads.wait_send()

    for i in range(1, n_ch):
        to_ch(i).wait_send()
    sent_slices(0, own)
    sent_slices(2, own_b)
    sent_slices(4, part)
    sent(6, others, n - 1)

    @pl.when(me < slices)
    def _():
        sent(1, prefix, n - 1)
        sent(3, suffix, n - 1)
        sent(5, parts, n - 1)


def hand_over(count, *refs):
    sources, targets, sems = refs[:count], refs[count : 2 * count], refs[-1]
    stores = [
        pltpu.make_async_copy(sources[i], targets[i], sems.at[i]) for i in range(count)
    ]
    for store in stores:
        store.start()
    for store in stores:
        store.wait()


def local(
    query_proj, key_proj, value_proj, key_taps, value_taps,
    residues, decay_rates, skip_weight, norm_gain, out_grad,
):
    rows, channels = key_proj.shape
    groups, modes = residues.shape
    group_size = channels // groups
    n, n_ch = lax.axis_size("ctx"), lax.axis_size("ch")
    slices = channels // TILE
    assert modes == group_size == 16 and slices <= n and rows == LANES
    field = max(LANES, groups)
    state = lambda count: pltpu.VMEM((count, group_size, TILE), BF16)
    whole = lambda kind: pltpu.VMEM((rows, channels), kind)
    vmem = pl.BlockSpec(memory_space=pltpu.VMEM)
    anywhere = pl.BlockSpec(memory_space=pl.ANY)
    shapes = (
        *([jax.ShapeDtypeStruct((rows, channels), BF16)] * 4),
        *([jax.ShapeDtypeStruct((3, groups), F32)] * 2),
        *([jax.ShapeDtypeStruct((1, channels), F32)] * 2),
    )
    results = pl.pallas_call(
        functools.partial(body, n, n_ch, slices, float(channels * n_ch), group_size),
        out_shape=tuple(pltpu.VMEM(shape.shape, shape.dtype) for shape in shapes),
        in_specs=[anywhere] * 3 + [vmem] * 6 + [anywhere],
        out_specs=(vmem,) * 8,
        scratch_shapes=[
            *([whole(BF16)] * 4), pltpu.SemaphoreType.DMA((4,)),
            pltpu.VMEM((40, field), F32), pltpu.VMEM((1, channels), F32),
            pltpu.VMEM((4, channels), F32), pltpu.VMEM((4, channels), F32),
            pltpu.VMEM((4, channels), F32), pltpu.VMEM((4, channels), F32),
            pltpu.VMEM((2, 16, channels), F32), pltpu.VMEM((2, 8, channels), F32),
            pltpu.VMEM((8, channels), F32),
            pltpu.VMEM((2 * rows, channels), BF16), pltpu.VMEM((2 * rows, channels), BF16),
            pltpu.VMEM((channels, 2 * rows), BF16), pltpu.VMEM((channels, 2 * rows), BF16),
            pltpu.VMEM((groups, rows), F32), pltpu.VMEM((groups, rows), F32),
            pltpu.VMEM((TILE, TILE), BF16),
            whole(BF16), whole(F32), whole(F32), whole(F32), whole(BF16),
            whole(BF16), whole(BF16), pltpu.VMEM((slices * 16, TILE), BF16),
            state(slices), state(n), state(n), state(slices),
            state(slices), state(n), state(n), state(slices),
            pltpu.VMEM((slices, 2, TILE), F32), pltpu.VMEM((n, 2, TILE), F32),
            pltpu.VMEM((slices, 2, TILE), F32),
            pltpu.VMEM((8, field), F32), pltpu.VMEM((n, 8, field), F32),
            pltpu.VMEM((2, rows, LANES), F32), pltpu.VMEM((8, 2 * rows), F32),
            pltpu.VMEM((max(1, n_ch - 1), 8, 2 * rows), F32),
            pltpu.SemaphoreType.DMA((2,)), pltpu.SemaphoreType.DMA((2,)),
            pltpu.SemaphoreType.DMA((7,)), pltpu.SemaphoreType.DMA((7, n)),
            pltpu.SemaphoreType.DMA((max(1, n_ch - 1),)), pltpu.SemaphoreType.DMA((max(1, n_ch - 1),)),
        ],
        compiler_params=pltpu.CompilerParams(
            collective_id=0, has_side_effects=True, vmem_limit_bytes=54 << 20
        ),
        name="hyena",
    )(
        query_proj, key_proj, value_proj, key_taps.T, value_taps.T, residues.T, decay_rates.T,
        skip_weight.reshape(1, channels), norm_gain.reshape(1, channels), out_grad,
    )
    results = pl.pallas_call(
        functools.partial(hand_over, len(shapes)),
        out_shape=shapes,
        in_specs=[vmem] * len(shapes),
        out_specs=(anywhere,) * len(shapes),
        scratch_shapes=[pltpu.SemaphoreType.DMA((len(shapes),))],
        compiler_params=pltpu.CompilerParams(vmem_limit_bytes=32 << 20),
        name="hand_over",
    )(*(pltpu.with_memory_space_constraint(result, pltpu.VMEM) for result in results))
    return (
        *results[:4], results[4].T, results[5].T,
        results[6].reshape(channels), results[7].reshape(channels),
    )


def solution(mesh):
    wide = P("ctx", "ch")
    placed = (
        wide, wide, wide, P("ch", None), P("ch", None), P("ch", None), P("ch", None),
        P("ch"), P("ch"), wide,
    )
    return jax.shard_map(
        local, mesh=mesh, in_specs=placed,
        out_specs=(wide, wide, wide, wide, P("ch", None), P("ch", None), P("ch"), P("ch")),
        check_vma=False,
    )
```

```python
import functools

import jax
import jax.numpy as jnp
from jax import lax
from jax.experimental import pallas as pl
from jax.experimental.pallas import tpu as pltpu
from jax.sharding import PartitionSpec as P

EPSILON = 1e-06
TILE = 256
LANES = 128
CHUNK = 32
BATCH = 4
F32, BF16 = jnp.float32, jnp.bfloat16


def halves(wide):
    high = wide.astype(BF16)
    return high, (wide - high.astype(F32)).astype(BF16)


def body(
    n, n_ch, slices, width_all, group_size,
    q_hbm, k_hbm, v_hbm, kt_ref, vt_ref, res_ref, rates_ref, skip_ref, gain_ref, og_hbm,
    out_ref, qg_ref, kg_ref, vg_ref, ktg_ref, vtg_ref, skg_ref, gng_ref,
    q_ref, k_ref, v_ref, og_ref, io_sem, small, rate_line,
    tail_out, tail_in, head_out, head_in, before, last, taps,
    lag_up, lag_down, up_turned, down_turned, filt, turned, mask_half,
    prod, kmix, vmix, mixed, mgrad, kmg, vmg, tap_rows,
    own, gathered, prefix, incoming,
    own_b, gathered_b, suffix, incoming_b,
    part, parts, total, mine, others,
    row_acc, row_out, row_in,
    tail_sem, head_sem, send_sem, recv_sem, ch_send, ch_recv,
):
    me = lax.axis_index("ctx")
    me_ch = lax.axis_index("ch")
    rows = q_ref.shape[0]
    groups = rates_ref.shape[1]
    groups_tile = TILE // group_size
    groups_lanes = LANES // group_size
    load_k, load_v, load_q, load_og = (
        pltpu.make_async_copy(src, dst, io_sem.at[place])
        for place, (src, dst) in enumerate(
            ((k_hbm, k_ref), (v_hbm, v_ref), (q_hbm, q_ref), (og_hbm, og_ref))
        )
    )

    def to_ctx(src, dst, s_sem, r_sem, peer):
        return pltpu.make_async_remote_copy(
            src_ref=src, dst_ref=dst, send_sem=s_sem, recv_sem=r_sem,
            device_id={"ctx": peer}, device_id_type=pl.DeviceIdType.MESH,
        )

    def columns(j):
        return pl.ds(pl.multiple_of(j * TILE, TILE), TILE)

    def group_rows(j):
        return pl.ds(pl.multiple_of(j * groups_tile, groups_tile), groups_tile)

    def in_batches(first, last, order, work, before=None, after=None):
        batch = BATCH if first % BATCH == last % BATCH == 0 else 1

        @pl.loop(first // batch, last // batch)
        def _(b):
            places = [order(b * batch + u) for u in range(batch)]
            for j in places if before else ():
                before(j)
            for j in places:
                work(j)
            for j in places if after else ():
                after(j)

    def int_of(i):
        return i

    def in_turn(i):
        return lax.rem(me + i, slices)

    barrier = pltpu.get_barrier_semaphore()

    @pl.loop(1, n)
    def _(i):
        pl.semaphore_signal(
            barrier, inc=1, device_id={"ctx": lax.rem(me + i, n)},
            device_id_type=pl.DeviceIdType.MESH,
        )

    for i in range(1, n_ch):
        pl.semaphore_signal(
            barrier, inc=1, device_id={"ch": lax.rem(me_ch + i, n_ch)},
            device_id_type=pl.DeviceIdType.MESH,
        )
    for load in (load_k, load_v, load_q, load_og):
        load.start()

    lane = lax.broadcasted_iota(jnp.int32, (group_size, LANES), 1)
    sub = lax.broadcasted_iota(jnp.int32, (group_size, LANES), 0)
    lane_wide = lane.astype(F32)
    backwards = LANES - 1 - lane
    own_lane = sub == lax.rem(lane, group_size)
    small[...] = jnp.zeros(small.shape, F32)
    small[0:16, 0:groups] = rates_ref[...]
    small[16:32, 0:groups] = res_ref[...]
    small[32:35, 0:groups] = kt_ref[...].astype(F32)
    small[35:38, 0:groups] = vt_ref[...].astype(F32)

    def source_of(first):
        start = (first // LANES) * LANES
        return pl.ds(pl.multiple_of(start, LANES), LANES), first - start

    def pick(table, index):
        return jnp.take_along_axis(table, index, axis=1)

    def of_channels(kind, block):
        source, first = source_of(block * groups_lanes)
        return pick(small[kind, source], first + lane // group_size)

    def lines_of(block):
        cols = pl.ds(pl.multiple_of(block * LANES, LANES), LANES)
        source, first = source_of(block * groups_lanes)
        chosen = first + lane // group_size
        rates = pick(small[0:16, source], chosen)
        rate_line[0:1, cols] = jnp.sum(jnp.where(own_lane, rates, 0.0), axis=0, keepdims=True)
        taps[0:8, cols] = pick(small[32:40, source], chosen[0:8])

    in_batches(0, slices * TILE // LANES, int_of, lines_of)

    block_mask = (
        lax.broadcasted_iota(jnp.int32, (TILE, TILE), 0) // group_size
        == lax.broadcasted_iota(jnp.int32, (TILE, TILE), 1) // group_size
    )
    mask_half[...] = block_mask.astype(F32).astype(BF16)

    load_k.wait()
    load_v.wait()
    tail_out[0:2] = k_ref[rows - 16 : rows].astype(F32)[14:16]
    tail_out[2:4] = v_ref[rows - 16 : rows].astype(F32)[14:16]
    tails = to_ctx(tail_out, tail_in, tail_sem.at[0], tail_sem.at[1], lax.rem(me + 1, n))
    heads = to_ctx(head_out, head_in, head_sem.at[0], head_sem.at[1], lax.rem(me + n - 1, n))
    pl.semaphore_wait(barrier, n - 1 + n_ch - 1)

    @pl.when(me < n - 1)
    def _():
        tails.start()

    @pl.when(me == 0)
    def _():
        tail_in[...] = jnp.zeros(tail_in.shape, F32)

    row8 = lax.broadcasted_iota(jnp.int32, (8, TILE), 0).astype(F32)
    row_steps = lax.broadcasted_iota(jnp.int32, (rows // 8, TILE), 0).astype(F32) * 8.0

    def tables_of(j):
        cols = columns(j)
        rate = rate_line[0:1, cols]
        steps = jnp.exp(-rate * row_steps)
        up8 = jnp.exp(-rate * row8)
        down8 = jnp.exp(-rate * (7.0 - row8))
        count = rows // 8
        for table, piece, order in (
            (lag_up, up8, range(count)), (lag_down, down8, reversed(range(count)))
        ):
            high, low = halves(jnp.concatenate([piece * steps[a : a + 1] for a in order], axis=0))
            table[0:rows, cols] = high
            table[rows : 2 * rows, cols] = low
        source, first = source_of(j * groups_tile)
        rates, residues = small[0:16, source], small[16:32, source]
        lines = []
        for g in range(groups_tile):
            index = jnp.broadcast_to(first + g, (group_size, LANES))
            fade = jnp.exp(-pick(rates, index) * lane_wide)
            lines.append(jnp.sum(pick(residues, index) * fade, axis=0, keepdims=True))
            at = pl.ds(pl.multiple_of(j * TILE + g * group_size, group_size), group_size)
            for table, wide in ((up_turned, fade), (down_turned, pick(fade, backwards))):
                high, low = halves(wide)
                table[at, 0:LANES] = high
                table[at, LANES : 2 * LANES] = low
        lines = jnp.concatenate(lines, axis=0)
        filt[group_rows(j), :] = lines
        turned[group_rows(j), :] = pick(lines, backwards)

    in_batches(0, slices, int_of, tables_of)

    lane_group = lax.broadcasted_iota(jnp.int32, (CHUNK, TILE), 1) // group_size
    tri_row = lax.broadcasted_iota(jnp.int32, (rows, rows), 0)
    tri_col = lax.broadcasted_iota(jnp.int32, (rows, rows), 1)

    @pl.when(me > 0)
    def _():
        tails.wait_recv()

    before[0, 14:16] = tail_in[0:2]
    before[1, 14:16] = tail_in[2:4]

    def delayed(ref, cols, which, r):
        if r == 0:
            wide = jnp.concatenate([before[which, :, cols], ref[0:CHUNK, cols].astype(F32)], axis=0)
        else:
            wide = ref[r - 16 : r + CHUNK, cols].astype(F32)
        return wide[16 : 16 + CHUNK], wide[15 : 15 + CHUNK], wide[14 : 14 + CHUNK]

    def mix(parts_of, cols, base):
        zero, one, two = parts_of
        return (
            zero * taps[base : base + 1, cols]
            + one * taps[base + 1 : base + 2, cols]
            + two * taps[base + 2 : base + 3, cols]
        )

    def folded(x):
        return jnp.sum(x.reshape(x.shape[0] // 8, 8, TILE), axis=0)

    def modal(table, j, signal):
        full = jnp.dot(
            table[columns(j), :], jnp.concatenate([signal, signal], axis=0),
            preferred_element_type=F32,
        )
        kept = jnp.where(block_mask, full, 0.0)
        return jnp.sum(kept.reshape(groups_tile, group_size, TILE), axis=0).astype(BF16)

    def spread(table, cols, state):
        big = jnp.concatenate([state] * groups_tile, axis=0) * mask_half[...]
        return jnp.dot(
            jnp.concatenate([table[0:rows, cols], table[rows : 2 * rows, cols]], axis=1),
            jnp.concatenate([big, big], axis=0),
            preferred_element_type=F32,
        )

    def toeplitz(table, shift, j, ref, cols, keep):
        lines = table[group_rows(j), :]
        lhs, rhs = [], []
        for g in range(groups_tile):
            spread_line = jnp.broadcast_to(lines[g : g + 1, :], (rows, rows))
            turned_line = pltpu.roll(spread_line, shift, 1, stride=1, stride_axis=0)
            lhs.append(jnp.where(keep, turned_line, 0.0).astype(BF16))
            for r in range(0, rows, CHUNK):
                wide = ref[r : r + CHUNK, cols].astype(F32)
                rhs.append(jnp.where(lane_group == g, wide, 0.0).astype(BF16))
        return jnp.dot(
            jnp.concatenate(lhs, axis=1), jnp.concatenate(rhs, axis=0),
            preferred_element_type=F32,
        )

    def scatter(phase, source, target, j):
        copy = to_ctx(
            source.at[j], target.at[me], send_sem.at[phase], recv_sem.at[phase, me], j
        )

        @pl.when(j != me)
        def _():
            copy.start()

        @pl.when(j == me)
        def _():
            target[me] = source[j]

    def arrive(phase, source, target, i):
        @pl.when(i != me)
        def _():
            to_ctx(
                source.at[0], target.at[i], send_sem.at[phase], recv_sem.at[phase, i], i
            ).wait_recv()

    def sent(phase, source, count):
        if count:
            whole = source.at[pl.ds(0, count)]
            pltpu.make_async_copy(whole, whole, send_sem.at[phase]).wait()

    def sent_slices(phase, source):
        if n == slices:
            sent(phase, source, slices - 1)
        else:
            @pl.when(me < slices)
            def _():
                sent(phase, source, slices - 1)

            @pl.when(me >= slices)
            def _():
                sent(phase, source, slices)

    def of_owner():
        rate, residue = (
            jnp.concatenate([of_channels(kind, 2 * me), of_channels(kind, 2 * me + 1)], axis=1)
            for kind in (slice(0, 16), slice(16, 32))
        )
        return jnp.exp(-rate * float(rows)), residue * jnp.exp(-rate)

    def mix_tile(j):
        cols = columns(j)
        for r in range(0, rows, CHUNK):
            part_rows = slice(r, r + CHUNK)
            key = mix(delayed(k_ref, cols, 0, r), cols, 0)
            value = mix(delayed(v_ref, cols, 1, r), cols, 3)
            kmix[part_rows, cols] = key
            vmix[part_rows, cols] = value
            prod[part_rows, cols] = (key * value).astype(BF16)
        own[j] = modal(down_turned, j, prod[:, cols])

    in_batches(
        0, slices, in_turn, mix_tile, after=lambda j: scatter(0, own, gathered, j)
    )

    def long_forward(j):
        cols = columns(j)
        mixed[:, cols] = toeplitz(turned, 1, j, prod, cols, tri_row >= tri_col)

    early = slices // 2

    in_batches(0, early, int_of, long_forward)

    @pl.when(me < slices)
    def _():
        fall, scale = of_owner()

        def step(i, carry):
            prefix[i] = (carry * scale).astype(BF16)
            scatter(1, prefix, incoming, i)
            arrive(0, own, gathered, i)
            return fall * carry + gathered[i].astype(F32)

        lax.fori_loop(0, n, step, jnp.zeros((group_size, TILE), F32))

    in_batches(early, slices, int_of, long_forward)

    row_acc[...] = jnp.zeros(row_acc.shape, F32)
    load_q.wait()
    load_og.wait()

    def gate_tile(j):
        cols = columns(j)
        mixed[:, cols] += spread(lag_up, cols, incoming[j])
        for r in range(0, rows, CHUNK):
            part_rows = slice(r, r + CHUNK)
            full = mixed[part_rows, cols] + skip_ref[0:1, cols] * prod[part_rows, cols].astype(F32)
            mixed[part_rows, cols] = full
            gated = q_ref[part_rows, cols].astype(F32) * full
            squares = gated * gated
            along = gated * gain_ref[0:1, cols] * og_ref[part_rows, cols].astype(F32)
            row_acc[0, part_rows] += squares[:, :128] + squares[:, 128:]
            row_acc[1, part_rows] += along[:, :128] + along[:, 128:]

    in_batches(
        0, slices, in_turn, gate_tile, before=lambda j: arrive(1, prefix, incoming, j)
    )

    both = row_acc[...].reshape(2 * rows, LANES)
    high, low = halves(both)
    lowest = (both - high.astype(F32) - low.astype(F32)).astype(BF16)
    row_out[...] = lax.dot_general(
        jnp.ones((16, 3 * LANES), BF16), jnp.concatenate([high, low, lowest], axis=1),
        (((1,), (1,)), ((), ())), preferred_element_type=F32,
    )[0:8]

    def to_ch(i):
        return pltpu.make_async_remote_copy(
            src_ref=row_out, dst_ref=row_in.at[i - 1], send_sem=ch_send.at[i - 1],
            recv_sem=ch_recv.at[i - 1], device_id={"ch": lax.rem(me_ch + i, n_ch)},
            device_id_type=pl.DeviceIdType.MESH,
        )

    for i in range(1, n_ch):
        to_ch(i).start()
    summed = row_out[...]
    for i in range(1, n_ch):
        to_ch(i).wait_recv()
        summed = summed + row_in[i - 1]
    squares, along = summed[:, 0:rows], summed[:, rows : 2 * rows]
    scaled = lax.rsqrt(squares / width_all + EPSILON)
    pull = scaled * scaled * scaled * along / width_all
    row_acc[0] = jnp.broadcast_to(scaled[0:1], (rows, rows)).T
    row_acc[1] = jnp.broadcast_to(pull[0:1], (rows, rows)).T

    def grad_tile(j):
        cols = columns(j)
        gain = gain_ref[0:1, cols]
        skip_sum = gain_sum = jnp.zeros((8, TILE), F32)
        for r in range(0, rows, CHUNK):
            part_rows = slice(r, r + CHUNK)
            scaled = jnp.concatenate([row_acc[0, part_rows]] * 2, axis=1)
            pull = jnp.concatenate([row_acc[1, part_rows]] * 2, axis=1)
            query = q_ref[part_rows, cols].astype(F32)
            grad = og_ref[part_rows, cols].astype(F32)
            full = mixed[part_rows, cols]
            gated = query * full
            normed = gated * scaled
            out_ref[part_rows, cols] = (normed * gain).astype(BF16)
            gated_grad = scaled * gain * grad - gated * pull
            qg_ref[part_rows, cols] = (gated_grad * full).astype(BF16)
            mixed_grad = (gated_grad * query).astype(BF16)
            mgrad[part_rows, cols] = mixed_grad
            skip_sum += folded(mixed_grad.astype(F32) * prod[part_rows, cols].astype(F32))
            gain_sum += folded(grad * normed)
        own_b[j] = modal(up_turned, j, mgrad[:, cols])
        part[j, 0:1, :] = jnp.sum(skip_sum, axis=0, keepdims=True)
        part[j, 1:2, :] = jnp.sum(gain_sum, axis=0, keepdims=True)

    def send_grad_sums(j):
        scatter(2, own_b, gathered_b, j)
        scatter(4, part, parts, j)

    in_batches(0, slices, in_turn, grad_tile, after=send_grad_sums)

    def long_backward(j):
        cols = columns(j)
        mixed[:, cols] = toeplitz(filt, 0, j, mgrad, cols, tri_row <= tri_col)

    in_batches(0, early, int_of, long_backward)

    @pl.when(me < slices)
    def _():
        fall, scale = of_owner()

        def step(i, carry):
            place = n - 1 - i
            suffix[place] = (carry * scale).astype(BF16)
            scatter(3, suffix, incoming_b, place)
            arrive(2, own_b, gathered_b, place)
            return fall * carry + gathered_b[place].astype(F32)

        lax.fori_loop(0, n, step, jnp.zeros((group_size, TILE), F32))

        def add(i, carry):
            arrive(4, part, parts, i)
            return carry + parts[i]

        total[me] = lax.fori_loop(0, n, add, jnp.zeros((2, TILE), F32))

        @pl.loop(0, n)
        def _(i):
            @pl.when(i != me)
            def _():
                to_ctx(
                    total.at[me], total.at[me], send_sem.at[5], recv_sem.at[5, me], i
                ).start()

    in_batches(early, slices, int_of, long_backward)

    def final_tile(j):
        cols = columns(j)
        mixed[:, cols] += spread(lag_down, cols, incoming_b[j])
        sums = [jnp.zeros((8, TILE), F32)] * 6
        later = [jnp.zeros((8, TILE), F32)] * 2
        for r in reversed(range(0, rows, CHUNK)):
            part_rows = slice(r, r + CHUNK)
            pgrad = (
                mixed[part_rows, cols] + skip_ref[0:1, cols] * mgrad[part_rows, cols].astype(F32)
            )
            for which, (other, signal, target) in enumerate(
                ((vmix, k_ref, kmg), (kmix, v_ref, vmg))
            ):
                half = (pgrad * other[part_rows, cols]).astype(BF16)
                target[part_rows, cols] = half
                zero = half.astype(F32)
                wide = jnp.concatenate([zero, later[which]], axis=0)
                shifted = (zero, wide[1 : 1 + CHUNK], wide[2 : 2 + CHUNK])
                later[which] = zero[0:8]
                inside = signal[part_rows, cols].astype(F32)
                for offset in range(3):
                    place = 3 * which + offset
                    sums[place] = sums[place] + folded(shifted[offset] * inside)
        tap_sums = []
        for which in range(2):
            first, second = later[which][0:1], later[which][1:2]
            head_out[2 * which : 2 * which + 2, cols] = later[which][0:2]
            older = tail_in[2 * which : 2 * which + 1, cols]
            newer = tail_in[2 * which + 1 : 2 * which + 2, cols]
            edges = (0.0, first * newer, first * older + second * newer)
            for offset in range(3):
                tap_sums.append(
                    jnp.sum(sums[3 * which + offset], axis=0, keepdims=True) + edges[offset]
                )
        tap_sums = jnp.concatenate(tap_sums + [jnp.zeros((2, TILE), F32)], axis=0)
        high = tap_sums.astype(BF16).astype(F32)
        at = pl.ds(pl.multiple_of(j * 16, 16), 16)
        tap_rows[at, :] = jnp.concatenate([high, tap_sums - high], axis=0).astype(BF16)

    in_batches(
        0, slices, in_turn, final_tile, before=lambda j: arrive(3, suffix, incoming_b, j)
    )

    @pl.when(me > 0)
    def _():
        heads.start()

    @pl.when(me == n - 1)
    def _():
        head_in[...] = jnp.zeros(head_in.shape, F32)

    member = (
        lax.broadcasted_iota(jnp.int32, (TILE, LANES), 0) // group_size
        == lax.broadcasted_iota(jnp.int32, (TILE, LANES), 1)
    ).astype(F32).astype(BF16)
    grouped = jnp.dot(tap_rows[...], member, preferred_element_type=F32)
    fields = [jnp.zeros((8, LANES), F32)] * (mine.shape[1] // LANES)
    for j in range(slices):
        here = grouped[16 * j : 16 * j + 8] + grouped[16 * j + 8 : 16 * j + 16]
        field, start = divmod(j * groups_tile, LANES)
        fields[field] = fields[field] + (pltpu.roll(here, start, 1) if start else here)
    for field, value in enumerate(fields):
        mine[:, field * LANES : (field + 1) * LANES] = value

    @pl.loop(1, n)
    def _(i):
        to_ctx(
            mine, others.at[me], send_sem.at[6], recv_sem.at[6, me], lax.rem(me + i, n)
        ).start()

    def adjoint(j, r):
        cols = columns(j)
        for which, (source, target) in enumerate(((kmg, kg_ref), (vmg, vg_ref))):
            if r + CHUNK < rows:
                wide = source[r : r + CHUNK + 16, cols].astype(F32)
            else:
                wide = jnp.concatenate(
                    [source[r : r + CHUNK, cols].astype(F32), last[which, :, cols]], axis=0
                )
            shifted = (wide[0:CHUNK], wide[1 : 1 + CHUNK], wide[2 : 2 + CHUNK])
            target[r : r + CHUNK, cols] = mix(shifted, cols, 3 * which).astype(BF16)

    def adjoint_upper(j):
        for r in range(0, rows - CHUNK, CHUNK):
            adjoint(j, r)

    in_batches(0, slices, int_of, adjoint_upper)

    @pl.when(me < n - 1)
    def _():
        heads.wait_recv()

    last[0, 0:2] = head_in[0:2]
    last[1, 0:2] = head_in[2:4]

    in_batches(0, slices, int_of, lambda j: adjoint(j, rows - CHUNK))

    def arrive_total(j):
        @pl.when(j != me)
        def _():
            to_ctx(
                total.at[j], total.at[j], send_sem.at[5], recv_sem.at[5, j], j
            ).wait_recv()

    def totals_of(j):
        cols = columns(j)
        here = total[j]
        skg_ref[0:1, cols] = here[0:1]
        gng_ref[0:1, cols] = here[1:2]

    in_batches(0, slices, int_of, totals_of, before=arrive_total)

    others[me] = mine[...]

    def gather(i, carry):
        arrive(6, others, others, i)
        return carry + others[i]

    summed = lax.fori_loop(0, n, gather, jnp.zeros(mine.shape, F32))[:, 0:groups]
    ktg_ref[...] = summed[0:3]
    vtg_ref[...] = summed[3:6]

    @pl.when(me < n - 1)
    def _():
        tails.wait_send()

    @pl.when(me > 0)
    def _():
        heads.wait_send()

    for i in range(1, n_ch):
        to_ch(i).wait_send()
    sent_slices(0, own)
    sent_slices(2, own_b)
    sent_slices(4, part)
    sent(6, others, n - 1)

    @pl.when(me < slices)
    def _():
        sent(1, prefix, n - 1)
        sent(3, suffix, n - 1)
        sent(5, parts, n - 1)


def hand_over(count, *refs):
    sources, targets, sems = refs[:count], refs[count : 2 * count], refs[-1]
    stores = [
        pltpu.make_async_copy(sources[i], targets[i], sems.at[i]) for i in range(count)
    ]
    for store in stores:
        store.start()
    for store in stores:
        store.wait()


def local(
    query_proj, key_proj, value_proj, key_taps, value_taps,
    residues, decay_rates, skip_weight, norm_gain, out_grad,
):
    rows, channels = key_proj.shape
    groups, modes = residues.shape
    group_size = channels // groups
    n, n_ch = lax.axis_size("ctx"), lax.axis_size("ch")
    slices = channels // TILE
    assert modes == group_size == 16 and slices <= n and rows == LANES
    field = max(LANES, groups)
    state = lambda count: pltpu.VMEM((count, group_size, TILE), BF16)
    whole = lambda kind: pltpu.VMEM((rows, channels), kind)
    vmem = pl.BlockSpec(memory_space=pltpu.VMEM)
    anywhere = pl.BlockSpec(memory_space=pl.ANY)
    shapes = (
        *([jax.ShapeDtypeStruct((rows, channels), BF16)] * 4),
        *([jax.ShapeDtypeStruct((3, groups), F32)] * 2),
        *([jax.ShapeDtypeStruct((1, channels), F32)] * 2),
    )
    results = pl.pallas_call(
        functools.partial(body, n, n_ch, slices, float(channels * n_ch), group_size),
        out_shape=tuple(pltpu.VMEM(shape.shape, shape.dtype) for shape in shapes),
        in_specs=[anywhere] * 3 + [vmem] * 6 + [anywhere],
        out_specs=(vmem,) * 8,
        scratch_shapes=[
            *([whole(BF16)] * 4), pltpu.SemaphoreType.DMA((4,)),
            pltpu.VMEM((40, field), F32), pltpu.VMEM((1, channels), F32),
            pltpu.VMEM((4, channels), F32), pltpu.VMEM((4, channels), F32),
            pltpu.VMEM((4, channels), F32), pltpu.VMEM((4, channels), F32),
            pltpu.VMEM((2, 16, channels), F32), pltpu.VMEM((2, 8, channels), F32),
            pltpu.VMEM((8, channels), F32),
            pltpu.VMEM((2 * rows, channels), BF16), pltpu.VMEM((2 * rows, channels), BF16),
            pltpu.VMEM((channels, 2 * rows), BF16), pltpu.VMEM((channels, 2 * rows), BF16),
            pltpu.VMEM((groups, rows), F32), pltpu.VMEM((groups, rows), F32),
            pltpu.VMEM((TILE, TILE), BF16),
            whole(BF16), whole(F32), whole(F32), whole(F32), whole(BF16),
            whole(BF16), whole(BF16), pltpu.VMEM((slices * 16, TILE), BF16),
            state(slices), state(n), state(n), state(slices),
            state(slices), state(n), state(n), state(slices),
            pltpu.VMEM((slices, 2, TILE), F32), pltpu.VMEM((n, 2, TILE), F32),
            pltpu.VMEM((slices, 2, TILE), F32),
            pltpu.VMEM((8, field), F32), pltpu.VMEM((n, 8, field), F32),
            pltpu.VMEM((2, rows, LANES), F32), pltpu.VMEM((8, 2 * rows), F32),
            pltpu.VMEM((max(1, n_ch - 1), 8, 2 * rows), F32),
            pltpu.SemaphoreType.DMA((2,)), pltpu.SemaphoreType.DMA((2,)),
            pltpu.SemaphoreType.DMA((7,)), pltpu.SemaphoreType.DMA((7, n)),
            pltpu.SemaphoreType.DMA((max(1, n_ch - 1),)), pltpu.SemaphoreType.DMA((max(1, n_ch - 1),)),
        ],
        compiler_params=pltpu.CompilerParams(
            collective_id=0, has_side_effects=True, vmem_limit_bytes=54 << 20
        ),
        name="hyena",
    )(
        query_proj, key_proj, value_proj, key_taps.T, value_taps.T, residues.T, decay_rates.T,
        skip_weight.reshape(1, channels), norm_gain.reshape(1, channels), out_grad,
    )
    results = pl.pallas_call(
        functools.partial(hand_over, len(shapes)),
        out_shape=shapes,
        in_specs=[vmem] * len(shapes),
        out_specs=(anywhere,) * len(shapes),
        scratch_shapes=[pltpu.SemaphoreType.DMA((len(shapes),))],
        compiler_params=pltpu.CompilerParams(vmem_limit_bytes=32 << 20),
        name="hand_over",
    )(*(pltpu.with_memory_space_constraint(result, pltpu.VMEM) for result in results))
    return (
        *results[:4], results[4].T, results[5].T,
        results[6].reshape(channels), results[7].reshape(channels),
    )


def solution(mesh):
    wide = P("ctx", "ch")
    placed = (
        wide, wide, wide, P("ch", None), P("ch", None), P("ch", None), P("ch", None),
        P("ch"), P("ch"), wide,
    )
    return jax.shard_map(
        local, mesh=mesh, in_specs=placed,
        out_specs=(wide, wide, wide, wide, P("ch", None), P("ch", None), P("ch"), P("ch")),
        check_vma=False,
    )
```

```python
import functools

import jax
import jax.numpy as jnp
from jax import lax
from jax.experimental import pallas as pl
from jax.experimental.pallas import tpu as pltpu
from jax.sharding import PartitionSpec as P

EPSILON = 1e-06
TILE = 256
LANES = 128
CHUNK = 32
BATCH = 4
F32, BF16 = jnp.float32, jnp.bfloat16


def halves(wide):
    high = wide.astype(BF16)
    return high, (wide - high.astype(F32)).astype(BF16)


def body(
    n, n_ch, slices, width_all, group_size,
    q_hbm, k_hbm, v_hbm, kt_ref, vt_ref, res_ref, rates_ref, skip_ref, gain_ref, og_hbm,
    out_ref, qg_ref, kg_ref, vg_ref, ktg_ref, vtg_ref, skg_ref, gng_ref,
    q_ref, k_ref, v_ref, og_ref, k_end, v_end, io_sem, small, rate_line,
    tail_out, tail_in, head_out, head_in, before, last, taps,
    lag_up, lag_down, up_turned, down_turned, filt, turned, mask_half,
    prod, kmix, vmix, mixed, mgrad, kmg, vmg, tap_rows,
    own, gathered, prefix, incoming,
    own_b, gathered_b, suffix, incoming_b,
    part, parts, total, mine, others,
    row_acc, row_out, row_in,
    tail_sem, head_sem, send_sem, recv_sem, ch_send, ch_recv,
):
    me = lax.axis_index("ctx")
    me_ch = lax.axis_index("ch")
    rows = q_ref.shape[0]
    groups = rates_ref.shape[1]
    groups_tile = TILE // group_size
    groups_lanes = LANES // group_size
    load_k, load_v, load_q, load_og, load_k_end, load_v_end = (
        pltpu.make_async_copy(src, dst, io_sem.at[place])
        for place, (src, dst) in enumerate((
            (k_hbm, k_ref), (v_hbm, v_ref), (q_hbm, q_ref), (og_hbm, og_ref),
            (k_hbm.at[pl.ds(rows - 16, 16)], k_end), (v_hbm.at[pl.ds(rows - 16, 16)], v_end),
        ))
    )

    def to_ctx(src, dst, s_sem, r_sem, peer):
        return pltpu.make_async_remote_copy(
            src_ref=src, dst_ref=dst, send_sem=s_sem, recv_sem=r_sem,
            device_id={"ctx": peer}, device_id_type=pl.DeviceIdType.MESH,
        )

    def columns(j):
        return pl.ds(pl.multiple_of(j * TILE, TILE), TILE)

    def group_rows(j):
        return pl.ds(pl.multiple_of(j * groups_tile, groups_tile), groups_tile)

    def in_batches(first, last, order, work, before=None, after=None):
        batch = BATCH if first % BATCH == last % BATCH == 0 else 1

        @pl.loop(first // batch, last // batch)
        def _(b):
            places = [order(b * batch + u) for u in range(batch)]
            for j in places if before else ():
                before(j)
            for j in places:
                work(j)
            for j in places if after else ():
                after(j)

    def int_of(i):
        return i

    def in_turn(i):
        return lax.rem(me + i, slices)

    def own_last(i):
        return lax.rem(me + BATCH + i, slices)

    barrier = pltpu.get_barrier_semaphore()

    @pl.loop(1, n)
    def _(i):
        pl.semaphore_signal(
            barrier, inc=1, device_id={"ctx": lax.rem(me + i, n)},
            device_id_type=pl.DeviceIdType.MESH,
        )

    for i in range(1, n_ch):
        pl.semaphore_signal(
            barrier, inc=1, device_id={"ch": lax.rem(me_ch + i, n_ch)},
            device_id_type=pl.DeviceIdType.MESH,
        )
    for load in (load_k_end, load_v_end, load_k, load_v, load_q, load_og):
        load.start()

    lane = lax.broadcasted_iota(jnp.int32, (group_size, LANES), 1)
    sub = lax.broadcasted_iota(jnp.int32, (group_size, LANES), 0)
    lane_wide = lane.astype(F32)
    backwards = LANES - 1 - lane
    own_lane = sub == lax.rem(lane, group_size)
    small[...] = jnp.zeros(small.shape, F32)
    small[0:16, 0:groups] = rates_ref[...]
    small[16:32, 0:groups] = res_ref[...]
    small[32:35, 0:groups] = kt_ref[...].astype(F32)
    small[35:38, 0:groups] = vt_ref[...].astype(F32)

    def source_of(first):
        start = (first // LANES) * LANES
        return pl.ds(pl.multiple_of(start, LANES), LANES), first - start

    def pick(table, index):
        return jnp.take_along_axis(table, index, axis=1)

    def of_channels(kind, block):
        source, first = source_of(block * groups_lanes)
        return pick(small[kind, source], first + lane // group_size)

    def lines_of(block):
        cols = pl.ds(pl.multiple_of(block * LANES, LANES), LANES)
        source, first = source_of(block * groups_lanes)
        chosen = first + lane // group_size
        rates = pick(small[0:16, source], chosen)
        rate_line[0:1, cols] = jnp.sum(jnp.where(own_lane, rates, 0.0), axis=0, keepdims=True)
        taps[0:8, cols] = pick(small[32:40, source], chosen[0:8])

    in_batches(0, slices * TILE // LANES, int_of, lines_of)

    block_mask = (
        lax.broadcasted_iota(jnp.int32, (TILE, TILE), 0) // group_size
        == lax.broadcasted_iota(jnp.int32, (TILE, TILE), 1) // group_size
    )
    mask_half[...] = block_mask.astype(F32).astype(BF16)

    row8 = lax.broadcasted_iota(jnp.int32, (8, TILE), 0).astype(F32)
    row_steps = lax.broadcasted_iota(jnp.int32, (rows // 8, TILE), 0).astype(F32) * 8.0

    def of_groups(j):
        source, first = source_of(j * groups_tile)
        for g in range(groups_tile):
            index = jnp.broadcast_to(first + g, (group_size, LANES))
            at = pl.ds(pl.multiple_of(j * TILE + g * group_size, group_size), group_size)
            yield at, pick(small[0:16, source], index), pick(small[16:32, source], index)

    def store_halves(table, at, wide):
        high, low = halves(wide)
        table[at, 0:LANES] = high
        table[at, LANES : 2 * LANES] = low

    def down_turned_of(j):
        for at, rate, _ in of_groups(j):
            store_halves(down_turned, at, jnp.exp(-rate * backwards.astype(F32)))

    def filter_of(j):
        lines = []
        for at, rate, residue in of_groups(j):
            fade = jnp.exp(-rate * lane_wide)
            lines.append(jnp.sum(residue * fade, axis=0, keepdims=True))
            store_halves(up_turned, at, fade)
        lines = jnp.concatenate(lines, axis=0)
        filt[group_rows(j), :] = lines
        turned[group_rows(j), :] = pick(lines, backwards)

    def table_of(table, going_up, j):
        cols = columns(j)
        rate = rate_line[0:1, cols]
        steps = jnp.exp(-rate * row_steps)
        piece = jnp.exp(-rate * (row8 if going_up else 7.0 - row8))
        order = range(rows // 8) if going_up else reversed(range(rows // 8))
        high, low = halves(jnp.concatenate([piece * steps[a : a + 1] for a in order], axis=0))
        table[0:rows, cols] = high
        table[rows : 2 * rows, cols] = low

    in_batches(0, slices, int_of, down_turned_of)

    load_k_end.wait()
    load_v_end.wait()
    tail_out[0:2] = k_end[...].astype(F32)[14:16]
    tail_out[2:4] = v_end[...].astype(F32)[14:16]
    tails = to_ctx(tail_out, tail_in, tail_sem.at[0], tail_sem.at[1], lax.rem(me + 1, n))
    heads = to_ctx(head_out, head_in, head_sem.at[0], head_sem.at[1], lax.rem(me + n - 1, n))
    pl.semaphore_wait(barrier, n - 1 + n_ch - 1)

    @pl.when(me < n - 1)
    def _():
        tails.start()

    @pl.when(me == 0)
    def _():
        tail_in[...] = jnp.zeros(tail_in.shape, F32)

    lane_group = lax.broadcasted_iota(jnp.int32, (CHUNK, TILE), 1) // group_size
    tri_row = lax.broadcasted_iota(jnp.int32, (rows, rows), 0)
    tri_col = lax.broadcasted_iota(jnp.int32, (rows, rows), 1)

    def delayed(ref, cols, which, r):
        if r == 0:
            wide = jnp.concatenate([before[which, :, cols], ref[0:CHUNK, cols].astype(F32)], axis=0)
        else:
            wide = ref[r - 16 : r + CHUNK, cols].astype(F32)
        return wide[16 : 16 + CHUNK], wide[15 : 15 + CHUNK], wide[14 : 14 + CHUNK]

    def mix(parts_of, cols, base):
        zero, one, two = parts_of
        return (
            zero * taps[base : base + 1, cols]
            + one * taps[base + 1 : base + 2, cols]
            + two * taps[base + 2 : base + 3, cols]
        )

    def folded(x):
        return jnp.sum(x.reshape(x.shape[0] // 8, 8, TILE), axis=0)

    def modal(table, j, signal):
        full = jnp.dot(
            table[columns(j), :], jnp.concatenate([signal, signal], axis=0),
            preferred_element_type=F32,
        )
        kept = jnp.where(block_mask, full, 0.0)
        return jnp.sum(kept.reshape(groups_tile, group_size, TILE), axis=0).astype(BF16)

    def spread(table, cols, state):
        big = jnp.concatenate([state] * groups_tile, axis=0) * mask_half[...]
        return jnp.dot(
            jnp.concatenate([table[0:rows, cols], table[rows : 2 * rows, cols]], axis=1),
            jnp.concatenate([big, big], axis=0),
            preferred_element_type=F32,
        )

    def toeplitz(table, shift, j, ref, cols, keep):
        lines = table[group_rows(j), :]
        lhs, rhs = [], []
        for g in range(groups_tile):
            spread_line = jnp.broadcast_to(lines[g : g + 1, :], (rows, rows))
            turned_line = pltpu.roll(spread_line, shift, 1, stride=1, stride_axis=0)
            lhs.append(jnp.where(keep, turned_line, 0.0).astype(BF16))
            for r in range(0, rows, CHUNK):
                wide = ref[r : r + CHUNK, cols].astype(F32)
                rhs.append(jnp.where(lane_group == g, wide, 0.0).astype(BF16))
        return jnp.dot(
            jnp.concatenate(lhs, axis=1), jnp.concatenate(rhs, axis=0),
            preferred_element_type=F32,
        )

    def scatter(phase, source, target, j):
        copy = to_ctx(
            source.at[j], target.at[me], send_sem.at[phase], recv_sem.at[phase, me], j
        )

        @pl.when(j != me)
        def _():
            copy.start()

        @pl.when(j == me)
        def _():
            target[me] = source[j]

    def arrive(phase, source, target, i):
        @pl.when(i != me)
        def _():
            to_ctx(
                source.at[0], target.at[i], send_sem.at[phase], recv_sem.at[phase, i], i
            ).wait_recv()

    def sent(phase, source, count):
        if count:
            whole = source.at[pl.ds(0, count)]
            pltpu.make_async_copy(whole, whole, send_sem.at[phase]).wait()

    def sent_slices(phase, source):
        if n == slices:
            sent(phase, source, slices - 1)
        else:
            @pl.when(me < slices)
            def _():
                sent(phase, source, slices - 1)

            @pl.when(me >= slices)
            def _():
                sent(phase, source, slices)

    def of_owner():
        rate, residue = (
            jnp.concatenate([of_channels(kind, 2 * me), of_channels(kind, 2 * me + 1)], axis=1)
            for kind in (slice(0, 16), slice(16, 32))
        )
        return jnp.exp(-rate * float(rows)), residue * jnp.exp(-rate)

    def mix_rows(cols, r):
        part_rows = slice(r, r + CHUNK)
        key = mix(delayed(k_ref, cols, 0, r), cols, 0)
        value = mix(delayed(v_ref, cols, 1, r), cols, 3)
        kmix[part_rows, cols] = key
        vmix[part_rows, cols] = value
        prod[part_rows, cols] = (key * value).astype(BF16)

    def mix_lower(j):
        for r in range(CHUNK, rows, CHUNK):
            mix_rows(columns(j), r)

    def mix_tile(j):
        mix_rows(columns(j), 0)
        own[j] = modal(down_turned, j, prod[:, columns(j)])

    load_k.wait()
    load_v.wait()
    in_batches(0, slices, int_of, mix_lower)

    @pl.when(me > 0)
    def _():
        tails.wait_recv()

    before[0, 14:16] = tail_in[0:2]
    before[1, 14:16] = tail_in[2:4]
    in_batches(
        0, slices, own_last, mix_tile, after=lambda j: scatter(0, own, gathered, j)
    )

    def long_forward(j):
        cols = columns(j)
        mixed[:, cols] = toeplitz(turned, 1, j, prod, cols, tri_row >= tri_col)

    def scan(taken, own, gathered, given, prefix, incoming, order):
        group = BATCH if n % BATCH == 0 else 1

        @pl.when(me < slices)
        def _():
            fall, scale = of_owner()

            def step(b, carry):
                places = [order(b * group + u) for u in range(group)]
                for place in places:
                    arrive(taken, own, gathered, place)
                for place in places:
                    prefix[place] = (carry * scale).astype(BF16)
                    carry = fall * carry + gathered[place].astype(F32)
                for place in places:
                    scatter(given, prefix, incoming, place)
                return carry

            lax.fori_loop(0, n // group, step, jnp.zeros((group_size, TILE), F32))

    in_batches(0, slices, int_of, filter_of)
    in_batches(0, slices, int_of, functools.partial(table_of, lag_up, True))
    scan(0, own, gathered, 1, prefix, incoming, int_of)
    in_batches(0, slices, int_of, long_forward)

    row_acc[...] = jnp.zeros(row_acc.shape, F32)
    load_q.wait()
    load_og.wait()

    def gate_tile(j):
        cols = columns(j)
        mixed[:, cols] += spread(lag_up, cols, incoming[j])
        for r in range(0, rows, CHUNK):
            part_rows = slice(r, r + CHUNK)
            full = mixed[part_rows, cols] + skip_ref[0:1, cols] * prod[part_rows, cols].astype(F32)
            mixed[part_rows, cols] = full
            gated = q_ref[part_rows, cols].astype(F32) * full
            squares = gated * gated
            along = gated * gain_ref[0:1, cols] * og_ref[part_rows, cols].astype(F32)
            row_acc[0, part_rows] += squares[:, :128] + squares[:, 128:]
            row_acc[1, part_rows] += along[:, :128] + along[:, 128:]

    in_batches(
        0, slices, in_turn, gate_tile, before=lambda j: arrive(1, prefix, incoming, j)
    )

    both = row_acc[...].reshape(2 * rows, LANES)
    high, low = halves(both)
    lowest = (both - high.astype(F32) - low.astype(F32)).astype(BF16)
    row_out[...] = lax.dot_general(
        jnp.ones((16, 3 * LANES), BF16), jnp.concatenate([high, low, lowest], axis=1),
        (((1,), (1,)), ((), ())), preferred_element_type=F32,
    )[0:8]

    def to_ch(i):
        return pltpu.make_async_remote_copy(
            src_ref=row_out, dst_ref=row_in.at[i - 1], send_sem=ch_send.at[i - 1],
            recv_sem=ch_recv.at[i - 1], device_id={"ch": lax.rem(me_ch + i, n_ch)},
            device_id_type=pl.DeviceIdType.MESH,
        )

    for i in range(1, n_ch):
        to_ch(i).start()
    in_batches(0, slices, int_of, functools.partial(table_of, lag_down, False))
    summed = row_out[...]
    for i in range(1, n_ch):
        to_ch(i).wait_recv()
        summed = summed + row_in[i - 1]
    squares, along = summed[:, 0:rows], summed[:, rows : 2 * rows]
    scaled = lax.rsqrt(squares / width_all + EPSILON)
    pull = scaled * scaled * scaled * along / width_all
    row_acc[0] = jnp.broadcast_to(scaled[0:1], (rows, rows)).T
    row_acc[1] = jnp.broadcast_to(pull[0:1], (rows, rows)).T

    def gated_parts(part_rows, cols):
        scaled = jnp.concatenate([row_acc[0, part_rows]] * 2, axis=1)
        pull = jnp.concatenate([row_acc[1, part_rows]] * 2, axis=1)
        query = q_ref[part_rows, cols].astype(F32)
        grad = og_ref[part_rows, cols].astype(F32)
        full = mixed[part_rows, cols]
        gated = query * full
        gated_grad = scaled * gain_ref[0:1, cols] * grad - gated * pull
        return scaled, query, grad, full, gated, gated_grad

    def grad_tile(j):
        cols = columns(j)
        for r in range(0, rows, CHUNK):
            part_rows = slice(r, r + CHUNK)
            _, query, _, _, _, gated_grad = gated_parts(part_rows, cols)
            mgrad[part_rows, cols] = (gated_grad * query).astype(BF16)
        own_b[j] = modal(up_turned, j, mgrad[:, cols])

    def output_tile(j):
        cols = columns(j)
        skip_sum = gain_sum = jnp.zeros((8, TILE), F32)
        for r in range(0, rows, CHUNK):
            part_rows = slice(r, r + CHUNK)
            scaled, _, grad, full, gated, gated_grad = gated_parts(part_rows, cols)
            normed = gated * scaled
            out_ref[part_rows, cols] = (normed * gain_ref[0:1, cols]).astype(BF16)
            qg_ref[part_rows, cols] = (gated_grad * full).astype(BF16)
            skip_sum += folded(
                mgrad[part_rows, cols].astype(F32) * prod[part_rows, cols].astype(F32)
            )
            gain_sum += folded(grad * normed)
        part[j, 0:1, :] = jnp.sum(skip_sum, axis=0, keepdims=True)
        part[j, 1:2, :] = jnp.sum(gain_sum, axis=0, keepdims=True)

    in_batches(
        0, slices, own_last, grad_tile, after=lambda j: scatter(2, own_b, gathered_b, j)
    )
    in_batches(0, slices, own_last, output_tile, after=lambda j: scatter(4, part, parts, j))

    def long_backward(j):
        cols = columns(j)
        mixed[:, cols] = toeplitz(filt, 0, j, mgrad, cols, tri_row <= tri_col)

    scan(2, own_b, gathered_b, 3, suffix, incoming_b, lambda i: n - 1 - i)
    middle = slices // BATCH // 2 * BATCH
    in_batches(0, middle, int_of, long_backward)

    @pl.when(me < slices)
    def _():
        def add(i, carry):
            arrive(4, part, parts, i)
            return carry + parts[i]

        total[...] = lax.fori_loop(0, n, add, jnp.zeros((2, TILE), F32))

    in_batches(middle, slices, int_of, long_backward)

    def final_tile(j):
        cols = columns(j)
        mixed[:, cols] += spread(lag_down, cols, incoming_b[j])
        sums = [jnp.zeros((8, TILE), F32)] * 6
        later = [jnp.zeros((8, TILE), F32)] * 2
        for r in reversed(range(0, rows, CHUNK)):
            part_rows = slice(r, r + CHUNK)
            pgrad = (
                mixed[part_rows, cols] + skip_ref[0:1, cols] * mgrad[part_rows, cols].astype(F32)
            )
            for which, (other, signal, target) in enumerate(
                ((vmix, k_ref, kmg), (kmix, v_ref, vmg))
            ):
                half = (pgrad * other[part_rows, cols]).astype(BF16)
                target[part_rows, cols] = half
                zero = half.astype(F32)
                wide = jnp.concatenate([zero, later[which]], axis=0)
                shifted = (zero, wide[1 : 1 + CHUNK], wide[2 : 2 + CHUNK])
                later[which] = zero[0:8]
                inside = signal[part_rows, cols].astype(F32)
                for offset in range(3):
                    place = 3 * which + offset
                    sums[place] = sums[place] + folded(shifted[offset] * inside)
        tap_sums = []
        for which in range(2):
            first, second = later[which][0:1], later[which][1:2]
            head_out[2 * which : 2 * which + 2, cols] = later[which][0:2]
            older = tail_in[2 * which : 2 * which + 1, cols]
            newer = tail_in[2 * which + 1 : 2 * which + 2, cols]
            edges = (0.0, first * newer, first * older + second * newer)
            for offset in range(3):
                tap_sums.append(
                    jnp.sum(sums[3 * which + offset], axis=0, keepdims=True) + edges[offset]
                )
        tap_sums = jnp.concatenate(tap_sums + [jnp.zeros((2, TILE), F32)], axis=0)
        high = tap_sums.astype(BF16).astype(F32)
        at = pl.ds(pl.multiple_of(j * 16, 16), 16)
        tap_rows[at, :] = jnp.concatenate([high, tap_sums - high], axis=0).astype(BF16)

    in_batches(
        0, slices, in_turn, final_tile, before=lambda j: arrive(3, suffix, incoming_b, j)
    )

    @pl.when(me > 0)
    def _():
        heads.start()

    @pl.when(me == n - 1)
    def _():
        head_in[...] = jnp.zeros(head_in.shape, F32)

    member = (
        lax.broadcasted_iota(jnp.int32, (TILE, LANES), 0) // group_size
        == lax.broadcasted_iota(jnp.int32, (TILE, LANES), 1)
    ).astype(F32).astype(BF16)
    grouped = jnp.dot(tap_rows[...], member, preferred_element_type=F32)
    fields = [jnp.zeros((8, LANES), F32)] * (mine.shape[1] // LANES)
    for j in range(slices):
        here = grouped[16 * j : 16 * j + 8] + grouped[16 * j + 8 : 16 * j + 16]
        field, start = divmod(j * groups_tile, LANES)
        fields[field] = fields[field] + (pltpu.roll(here, start, 1) if start else here)
    for field, value in enumerate(fields):
        mine[:, field * LANES : (field + 1) * LANES] = value

    @pl.when(me < slices)
    def _():
        mine[6:8, 0:TILE] = total[...]

    @pl.loop(1, n)
    def _(i):
        to_ctx(
            mine, others.at[me], send_sem.at[5], recv_sem.at[5, me], lax.rem(me + i, n)
        ).start()

    def adjoint(j, r):
        cols = columns(j)
        for which, (source, target) in enumerate(((kmg, kg_ref), (vmg, vg_ref))):
            if r + CHUNK < rows:
                wide = source[r : r + CHUNK + 16, cols].astype(F32)
            else:
                wide = jnp.concatenate(
                    [source[r : r + CHUNK, cols].astype(F32), last[which, :, cols]], axis=0
                )
            shifted = (wide[0:CHUNK], wide[1 : 1 + CHUNK], wide[2 : 2 + CHUNK])
            target[r : r + CHUNK, cols] = mix(shifted, cols, 3 * which).astype(BF16)

    def adjoint_upper(j):
        for r in range(0, rows - CHUNK, CHUNK):
            adjoint(j, r)

    in_batches(0, slices, int_of, adjoint_upper)

    @pl.when(me < n - 1)
    def _():
        heads.wait_recv()

    last[0, 0:2] = head_in[0:2]
    last[1, 0:2] = head_in[2:4]

    in_batches(0, slices, int_of, lambda j: adjoint(j, rows - CHUNK))

    others[me] = mine[...]

    def gather(i, carry):
        arrive(5, others, others, i)
        return carry + others[i]

    summed = lax.fori_loop(0, n, gather, jnp.zeros(mine.shape, F32))[:, 0:groups]
    ktg_ref[...] = summed[0:3]
    vtg_ref[...] = summed[3:6]

    def totals_of(j):
        cols = columns(j)
        here = others[j]
        skg_ref[0:1, cols] = here[6:7, 0:TILE]
        gng_ref[0:1, cols] = here[7:8, 0:TILE]

    in_batches(0, slices, int_of, totals_of)

    @pl.when(me < n - 1)
    def _():
        tails.wait_send()

    @pl.when(me > 0)
    def _():
        heads.wait_send()

    for i in range(1, n_ch):
        to_ch(i).wait_send()
    sent_slices(0, own)
    sent_slices(2, own_b)
    sent_slices(4, part)
    sent(5, others, n - 1)

    @pl.when(me < slices)
    def _():
        sent(1, prefix, n - 1)
        sent(3, suffix, n - 1)


def hand_over(count, *refs):
    sources, targets, sems = refs[:count], refs[count : 2 * count], refs[-1]
    stores = [
        pltpu.make_async_copy(sources[i], targets[i], sems.at[i]) for i in range(count)
    ]
    for store in stores:
        store.start()
    for store in stores:
        store.wait()


def local(
    query_proj, key_proj, value_proj, key_taps, value_taps,
    residues, decay_rates, skip_weight, norm_gain, out_grad,
):
    rows, channels = key_proj.shape
    groups, modes = residues.shape
    group_size = channels // groups
    n, n_ch = lax.axis_size("ctx"), lax.axis_size("ch")
    slices = channels // TILE
    assert modes == group_size == 16 and slices <= n and rows == LANES
    field = max(LANES, groups)
    wide_field = max(TILE, field)
    state = lambda count: pltpu.VMEM((count, group_size, TILE), BF16)
    whole = lambda kind: pltpu.VMEM((rows, channels), kind)
    vmem = pl.BlockSpec(memory_space=pltpu.VMEM)
    anywhere = pl.BlockSpec(memory_space=pl.ANY)
    shapes = (
        *([jax.ShapeDtypeStruct((rows, channels), BF16)] * 4),
        *([jax.ShapeDtypeStruct((3, groups), F32)] * 2),
        *([jax.ShapeDtypeStruct((1, channels), F32)] * 2),
    )
    results = pl.pallas_call(
        functools.partial(body, n, n_ch, slices, float(channels * n_ch), group_size),
        out_shape=tuple(pltpu.VMEM(shape.shape, shape.dtype) for shape in shapes),
        in_specs=[anywhere] * 3 + [vmem] * 6 + [anywhere],
        out_specs=(vmem,) * 8,
        scratch_shapes=[
            *([whole(BF16)] * 4), *([pltpu.VMEM((16, channels), BF16)] * 2),
            pltpu.SemaphoreType.DMA((6,)),
            pltpu.VMEM((40, field), F32), pltpu.VMEM((1, channels), F32),
            pltpu.VMEM((4, channels), F32), pltpu.VMEM((4, channels), F32),
            pltpu.VMEM((4, channels), F32), pltpu.VMEM((4, channels), F32),
            pltpu.VMEM((2, 16, channels), F32), pltpu.VMEM((2, 8, channels), F32),
            pltpu.VMEM((8, channels), F32),
            pltpu.VMEM((2 * rows, channels), BF16), pltpu.VMEM((2 * rows, channels), BF16),
            pltpu.VMEM((channels, 2 * rows), BF16), pltpu.VMEM((channels, 2 * rows), BF16),
            pltpu.VMEM((groups, rows), F32), pltpu.VMEM((groups, rows), F32),
            pltpu.VMEM((TILE, TILE), BF16),
            whole(BF16), whole(F32), whole(F32), whole(F32), whole(BF16),
            whole(BF16), whole(BF16), pltpu.VMEM((slices * 16, TILE), BF16),
            state(slices), state(n), state(n), state(slices),
            state(slices), state(n), state(n), state(slices),
            pltpu.VMEM((slices, 2, TILE), F32), pltpu.VMEM((n, 2, TILE), F32),
            pltpu.VMEM((2, TILE), F32), pltpu.VMEM((8, wide_field), F32),
            pltpu.VMEM((n, 8, wide_field), F32),
            pltpu.VMEM((2, rows, LANES), F32), pltpu.VMEM((8, 2 * rows), F32),
            pltpu.VMEM((max(1, n_ch - 1), 8, 2 * rows), F32),
            pltpu.SemaphoreType.DMA((2,)), pltpu.SemaphoreType.DMA((2,)),
            pltpu.SemaphoreType.DMA((6,)), pltpu.SemaphoreType.DMA((6, n)),
            pltpu.SemaphoreType.DMA((max(1, n_ch - 1),)), pltpu.SemaphoreType.DMA((max(1, n_ch - 1),)),
        ],
        compiler_params=pltpu.CompilerParams(
            collective_id=0, has_side_effects=True, vmem_limit_bytes=54 << 20
        ),
        name="hyena",
    )(
        query_proj, key_proj, value_proj, key_taps.T, value_taps.T, residues.T, decay_rates.T,
        skip_weight.reshape(1, channels), norm_gain.reshape(1, channels), out_grad,
    )
    results = pl.pallas_call(
        functools.partial(hand_over, len(shapes)),
        out_shape=shapes,
        in_specs=[vmem] * len(shapes),
        out_specs=(anywhere,) * len(shapes),
        scratch_shapes=[pltpu.SemaphoreType.DMA((len(shapes),))],
        compiler_params=pltpu.CompilerParams(vmem_limit_bytes=32 << 20),
        name="hand_over",
    )(*(pltpu.with_memory_space_constraint(result, pltpu.VMEM) for result in results))
    return (
        *results[:4], results[4].T, results[5].T,
        results[6].reshape(channels), results[7].reshape(channels),
    )


def solution(mesh):
    wide = P("ctx", "ch")
    placed = (
        wide, wide, wide, P("ch", None), P("ch", None), P("ch", None), P("ch", None),
        P("ch"), P("ch"), wide,
    )
    return jax.shard_map(
        local, mesh=mesh, in_specs=placed,
        out_specs=(wide, wide, wide, wide, P("ch", None), P("ch", None), P("ch"), P("ch")),
        check_vma=False,
    )
```

```python
import functools

import jax
import jax.numpy as jnp
from jax import lax
from jax.experimental import pallas as pl
from jax.experimental.pallas import tpu as pltpu
from jax.sharding import PartitionSpec as P

EPSILON = 1e-06
TILE = 256
LANES = 128
CHUNK = 32
BATCH = 4
F32, BF16 = jnp.float32, jnp.bfloat16


def halves(wide):
    high = wide.astype(BF16)
    return high, (wide - high.astype(F32)).astype(BF16)


def body(
    n, n_ch, slices, width_all, group_size,
    q_hbm, k_hbm, v_hbm, kt_ref, vt_ref, res_ref, rates_ref, skip_ref, gain_ref, og_hbm,
    out_ref, qg_ref, kg_ref, vg_ref, ktg_ref, vtg_ref, skg_ref, gng_ref,
    q_ref, k_ref, v_ref, og_ref, k_end, v_end, io_sem, small, rate_line,
    tail_out, tail_in, head_out, head_in, before, last, taps,
    lag_up, lag_down, up_turned, down_turned, filt, turned, mask_half,
    prod, kmix, vmix, mixed, mgrad, kmg, vmg, tap_rows,
    own, gathered, prefix, incoming,
    own_b, gathered_b, suffix, incoming_b,
    part, parts, total, mine, others,
    row_acc, row_out, row_in,
    tail_sem, head_sem, send_sem, recv_sem, ch_send, ch_recv,
):
    me = lax.axis_index("ctx")
    me_ch = lax.axis_index("ch")
    rows = q_ref.shape[0]
    groups = rates_ref.shape[1]
    groups_tile = TILE // group_size
    groups_lanes = LANES // group_size
    load_k, load_v, load_q, load_og, load_k_end, load_v_end = (
        pltpu.make_async_copy(src, dst, io_sem.at[place])
        for place, (src, dst) in enumerate((
            (k_hbm, k_ref), (v_hbm, v_ref), (q_hbm, q_ref), (og_hbm, og_ref),
            (k_hbm.at[pl.ds(rows - 16, 16)], k_end), (v_hbm.at[pl.ds(rows - 16, 16)], v_end),
        ))
    )

    def to_ctx(src, dst, s_sem, r_sem, peer):
        return pltpu.make_async_remote_copy(
            src_ref=src, dst_ref=dst, send_sem=s_sem, recv_sem=r_sem,
            device_id={"ctx": peer}, device_id_type=pl.DeviceIdType.MESH,
        )

    def columns(j):
        return pl.ds(pl.multiple_of(j * TILE, TILE), TILE)

    def group_rows(j):
        return pl.ds(pl.multiple_of(j * groups_tile, groups_tile), groups_tile)

    def in_batches(first, last, order, work, before=None, after=None):
        batch = BATCH if first % BATCH == last % BATCH == 0 else 1

        @pl.loop(first // batch, last // batch)
        def _(b):
            places = [order(b * batch + u) for u in range(batch)]
            for j in places if before else ():
                before(j)
            for j in places:
                work(j)
            for j in places if after else ():
                after(j)

    def int_of(i):
        return i

    def in_turn(i):
        return lax.rem(me + i, slices)

    def own_last(i):
        return lax.rem(me + BATCH + i, slices)

    barrier = pltpu.get_barrier_semaphore()

    @pl.loop(1, n)
    def _(i):
        pl.semaphore_signal(
            barrier, inc=1, device_id={"ctx": lax.rem(me + i, n)},
            device_id_type=pl.DeviceIdType.MESH,
        )

    for i in range(1, n_ch):
        pl.semaphore_signal(
            barrier, inc=1, device_id={"ch": lax.rem(me_ch + i, n_ch)},
            device_id_type=pl.DeviceIdType.MESH,
        )
    for load in (load_k_end, load_v_end, load_k, load_v, load_q, load_og):
        load.start()

    lane = lax.broadcasted_iota(jnp.int32, (group_size, LANES), 1)
    sub = lax.broadcasted_iota(jnp.int32, (group_size, LANES), 0)
    lane_wide = lane.astype(F32)
    backwards = LANES - 1 - lane
    own_lane = sub == lax.rem(lane, group_size)
    small[...] = jnp.zeros(small.shape, F32)
    small[0:16, 0:groups] = rates_ref[...]
    small[16:32, 0:groups] = res_ref[...]
    small[32:35, 0:groups] = kt_ref[...].astype(F32)
    small[35:38, 0:groups] = vt_ref[...].astype(F32)

    def source_of(first):
        start = (first // LANES) * LANES
        return pl.ds(pl.multiple_of(start, LANES), LANES), first - start

    def pick(table, index):
        return jnp.take_along_axis(table, index, axis=1)

    def of_channels(kind, block):
        source, first = source_of(block * groups_lanes)
        return pick(small[kind, source], first + lane // group_size)

    def lines_of(block):
        cols = pl.ds(pl.multiple_of(block * LANES, LANES), LANES)
        source, first = source_of(block * groups_lanes)
        chosen = first + lane // group_size
        rates = pick(small[0:16, source], chosen)
        rate_line[0:1, cols] = jnp.sum(jnp.where(own_lane, rates, 0.0), axis=0, keepdims=True)
        taps[0:8, cols] = pick(small[32:40, source], chosen[0:8])

    in_batches(0, slices * TILE // LANES, int_of, lines_of)

    block_mask = (
        lax.broadcasted_iota(jnp.int32, (TILE, TILE), 0) // group_size
        == lax.broadcasted_iota(jnp.int32, (TILE, TILE), 1) // group_size
    )
    mask_half[...] = block_mask.astype(F32).astype(BF16)

    row8 = lax.broadcasted_iota(jnp.int32, (8, TILE), 0).astype(F32)
    row_steps = lax.broadcasted_iota(jnp.int32, (rows // 8, TILE), 0).astype(F32) * 8.0

    def of_groups(j):
        source, first = source_of(j * groups_tile)
        for g in range(groups_tile):
            index = jnp.broadcast_to(first + g, (group_size, LANES))
            at = pl.ds(pl.multiple_of(j * TILE + g * group_size, group_size), group_size)
            yield at, pick(small[0:16, source], index), pick(small[16:32, source], index)

    def down_turned_of(j):
        for at, rate, _ in of_groups(j):
            down_turned[at, :] = jnp.exp(-rate * backwards.astype(F32)).astype(BF16)

    def filter_of(j):
        lines = []
        for at, rate, residue in of_groups(j):
            fade = jnp.exp(-rate * lane_wide)
            lines.append(jnp.sum(residue * fade, axis=0, keepdims=True))
            up_turned[at, :] = fade.astype(BF16)
        lines = jnp.concatenate(lines, axis=0)
        filt[group_rows(j), :] = lines
        turned[group_rows(j), :] = pick(lines, backwards)

    def table_of(table, going_up, j):
        cols = columns(j)
        rate = rate_line[0:1, cols]
        steps = jnp.exp(-rate * row_steps)
        piece = jnp.exp(-rate * (row8 if going_up else 7.0 - row8))
        order = range(rows // 8) if going_up else reversed(range(rows // 8))
        table[:, cols] = jnp.concatenate(
            [piece * steps[a : a + 1] for a in order], axis=0
        ).astype(BF16)

    in_batches(0, slices, int_of, down_turned_of)

    load_k_end.wait()
    load_v_end.wait()
    tail_out[0:2] = k_end[...].astype(F32)[14:16]
    tail_out[2:4] = v_end[...].astype(F32)[14:16]
    tails = to_ctx(tail_out, tail_in, tail_sem.at[0], tail_sem.at[1], lax.rem(me + 1, n))
    heads = to_ctx(head_out, head_in, head_sem.at[0], head_sem.at[1], lax.rem(me + n - 1, n))
    pl.semaphore_wait(barrier, n - 1 + n_ch - 1)

    @pl.when(me < n - 1)
    def _():
        tails.start()

    @pl.when(me == 0)
    def _():
        tail_in[...] = jnp.zeros(tail_in.shape, F32)

    lane_group = lax.broadcasted_iota(jnp.int32, (CHUNK, TILE), 1) // group_size
    tri_row = lax.broadcasted_iota(jnp.int32, (rows, rows), 0)
    tri_col = lax.broadcasted_iota(jnp.int32, (rows, rows), 1)

    def delayed(ref, cols, which, r):
        if r == 0:
            wide = jnp.concatenate([before[which, :, cols], ref[0:CHUNK, cols].astype(F32)], axis=0)
        else:
            wide = ref[r - 16 : r + CHUNK, cols].astype(F32)
        return wide[16 : 16 + CHUNK], wide[15 : 15 + CHUNK], wide[14 : 14 + CHUNK]

    def mix(parts_of, cols, base):
        zero, one, two = parts_of
        return (
            zero * taps[base : base + 1, cols]
            + one * taps[base + 1 : base + 2, cols]
            + two * taps[base + 2 : base + 3, cols]
        )

    def folded(x):
        return jnp.sum(x.reshape(x.shape[0] // 8, 8, TILE), axis=0)

    def modal(table, j, signal):
        full = jnp.dot(table[columns(j), :], signal, preferred_element_type=F32)
        kept = jnp.where(block_mask, full, 0.0)
        return jnp.sum(kept.reshape(groups_tile, group_size, TILE), axis=0).astype(BF16)

    def spread(table, cols, state):
        big = jnp.concatenate([state] * groups_tile, axis=0) * mask_half[...]
        return jnp.dot(table[:, cols], big, preferred_element_type=F32)

    def toeplitz(table, shift, j, ref, cols, keep):
        lines = table[group_rows(j), :]
        lhs, rhs = [], []
        for g in range(groups_tile):
            spread_line = jnp.broadcast_to(lines[g : g + 1, :], (rows, rows))
            turned_line = pltpu.roll(spread_line, shift, 1, stride=1, stride_axis=0)
            lhs.append(jnp.where(keep, turned_line, 0.0).astype(BF16))
            for r in range(0, rows, CHUNK):
                wide = ref[r : r + CHUNK, cols].astype(F32)
                rhs.append(jnp.where(lane_group == g, wide, 0.0).astype(BF16))
        return jnp.dot(
            jnp.concatenate(lhs, axis=1), jnp.concatenate(rhs, axis=0),
            preferred_element_type=F32,
        )

    def scatter(phase, source, target, j):
        copy = to_ctx(
            source.at[j], target.at[me], send_sem.at[phase], recv_sem.at[phase, me], j
        )

        @pl.when(j != me)
        def _():
            copy.start()

        @pl.when(j == me)
        def _():
            target[me] = source[j]

    def arrive(phase, source, target, i):
        @pl.when(i != me)
        def _():
            to_ctx(
                source.at[0], target.at[i], send_sem.at[phase], recv_sem.at[phase, i], i
            ).wait_recv()

    def sent(phase, source, count):
        if count:
            whole = source.at[pl.ds(0, count)]
            pltpu.make_async_copy(whole, whole, send_sem.at[phase]).wait()

    def sent_slices(phase, source):
        if n == slices:
            sent(phase, source, slices - 1)
        else:
            @pl.when(me < slices)
            def _():
                sent(phase, source, slices - 1)

            @pl.when(me >= slices)
            def _():
                sent(phase, source, slices)

    def of_owner():
        rate, residue = (
            jnp.concatenate([of_channels(kind, 2 * me), of_channels(kind, 2 * me + 1)], axis=1)
            for kind in (slice(0, 16), slice(16, 32))
        )
        return jnp.exp(-rate * float(rows)), residue * jnp.exp(-rate)

    def mix_rows(cols, r):
        part_rows = slice(r, r + CHUNK)
        key = mix(delayed(k_ref, cols, 0, r), cols, 0)
        value = mix(delayed(v_ref, cols, 1, r), cols, 3)
        kmix[part_rows, cols] = key
        vmix[part_rows, cols] = value
        prod[part_rows, cols] = (key * value).astype(BF16)

    def mix_lower(j):
        for r in range(CHUNK, rows, CHUNK):
            mix_rows(columns(j), r)

    def mix_tile(j):
        mix_rows(columns(j), 0)
        own[j] = modal(down_turned, j, prod[:, columns(j)])

    load_k.wait()
    load_v.wait()
    in_batches(0, slices, int_of, mix_lower)

    @pl.when(me > 0)
    def _():
        tails.wait_recv()

    before[0, 14:16] = tail_in[0:2]
    before[1, 14:16] = tail_in[2:4]
    in_batches(
        0, slices, own_last, mix_tile, after=lambda j: scatter(0, own, gathered, j)
    )

    def long_forward(j):
        cols = columns(j)
        mixed[:, cols] = toeplitz(turned, 1, j, prod, cols, tri_row >= tri_col)

    def scan(taken, own, gathered, given, prefix, incoming, order):
        group = BATCH if n % BATCH == 0 else 1

        @pl.when(me < slices)
        def _():
            fall, scale = of_owner()

            def step(b, carry):
                places = [order(b * group + u) for u in range(group)]
                for place in places:
                    arrive(taken, own, gathered, place)
                for place in places:
                    prefix[place] = (carry * scale).astype(BF16)
                    carry = fall * carry + gathered[place].astype(F32)
                for place in places:
                    scatter(given, prefix, incoming, place)
                return carry

            lax.fori_loop(0, n // group, step, jnp.zeros((group_size, TILE), F32))

    in_batches(0, slices, int_of, filter_of)
    in_batches(0, slices, int_of, functools.partial(table_of, lag_up, True))
    scan(0, own, gathered, 1, prefix, incoming, int_of)
    in_batches(0, slices, int_of, long_forward)

    row_acc[...] = jnp.zeros(row_acc.shape, F32)
    load_q.wait()
    load_og.wait()

    def gate_tile(j):
        cols = columns(j)
        far = spread(lag_up, cols, incoming[j])
        for r in range(0, rows, CHUNK):
            part_rows = slice(r, r + CHUNK)
            full = (
                mixed[part_rows, cols] + far[part_rows]
                + skip_ref[0:1, cols] * prod[part_rows, cols].astype(F32)
            )
            mixed[part_rows, cols] = full
            gated = q_ref[part_rows, cols].astype(F32) * full
            squares = gated * gated
            along = gated * gain_ref[0:1, cols] * og_ref[part_rows, cols].astype(F32)
            row_acc[0, part_rows] += squares[:, :128] + squares[:, 128:]
            row_acc[1, part_rows] += along[:, :128] + along[:, 128:]

    in_batches(
        0, slices, in_turn, gate_tile, before=lambda j: arrive(1, prefix, incoming, j)
    )

    both = row_acc[...].reshape(2 * rows, LANES)
    high, low = halves(both)
    lowest = (both - high.astype(F32) - low.astype(F32)).astype(BF16)
    row_out[...] = lax.dot_general(
        jnp.ones((16, 3 * LANES), BF16), jnp.concatenate([high, low, lowest], axis=1),
        (((1,), (1,)), ((), ())), preferred_element_type=F32,
    )[0:8]

    def to_ch(i):
        return pltpu.make_async_remote_copy(
            src_ref=row_out, dst_ref=row_in.at[i - 1], send_sem=ch_send.at[i - 1],
            recv_sem=ch_recv.at[i - 1], device_id={"ch": lax.rem(me_ch + i, n_ch)},
            device_id_type=pl.DeviceIdType.MESH,
        )

    for i in range(1, n_ch):
        to_ch(i).start()
    in_batches(0, slices, int_of, functools.partial(table_of, lag_down, False))
    summed = row_out[...]
    for i in range(1, n_ch):
        to_ch(i).wait_recv()
        summed = summed + row_in[i - 1]
    squares, along = summed[:, 0:rows], summed[:, rows : 2 * rows]
    scaled = lax.rsqrt(squares / width_all + EPSILON)
    pull = scaled * scaled * scaled * along / width_all
    row_acc[0] = jnp.broadcast_to(scaled[0:1], (rows, rows)).T
    row_acc[1] = jnp.broadcast_to(pull[0:1], (rows, rows)).T

    def gated_parts(part_rows, cols):
        scaled = jnp.concatenate([row_acc[0, part_rows]] * 2, axis=1)
        pull = jnp.concatenate([row_acc[1, part_rows]] * 2, axis=1)
        query = q_ref[part_rows, cols].astype(F32)
        grad = og_ref[part_rows, cols].astype(F32)
        full = mixed[part_rows, cols]
        gated = query * full
        gated_grad = scaled * gain_ref[0:1, cols] * grad - gated * pull
        return scaled, query, grad, full, gated, gated_grad

    def grad_tile(j):
        cols = columns(j)
        for r in range(0, rows, CHUNK):
            part_rows = slice(r, r + CHUNK)
            _, query, _, _, _, gated_grad = gated_parts(part_rows, cols)
            mgrad[part_rows, cols] = (gated_grad * query).astype(BF16)
        own_b[j] = modal(up_turned, j, mgrad[:, cols])

    def output_tile(j):
        cols = columns(j)
        skip_sum = gain_sum = jnp.zeros((8, TILE), F32)
        for r in range(0, rows, CHUNK):
            part_rows = slice(r, r + CHUNK)
            scaled, _, grad, full, gated, gated_grad = gated_parts(part_rows, cols)
            normed = gated * scaled
            out_ref[part_rows, cols] = (normed * gain_ref[0:1, cols]).astype(BF16)
            qg_ref[part_rows, cols] = (gated_grad * full).astype(BF16)
            skip_sum += folded(
                mgrad[part_rows, cols].astype(F32) * prod[part_rows, cols].astype(F32)
            )
            gain_sum += folded(grad * normed)
        part[j, 0:1, :] = jnp.sum(skip_sum, axis=0, keepdims=True)
        part[j, 1:2, :] = jnp.sum(gain_sum, axis=0, keepdims=True)

    in_batches(
        0, slices, own_last, grad_tile, after=lambda j: scatter(2, own_b, gathered_b, j)
    )
    in_batches(0, slices, own_last, output_tile, after=lambda j: scatter(4, part, parts, j))

    def long_backward(j):
        cols = columns(j)
        mixed[:, cols] = toeplitz(filt, 0, j, mgrad, cols, tri_row <= tri_col)

    scan(2, own_b, gathered_b, 3, suffix, incoming_b, lambda i: n - 1 - i)
    middle = slices // BATCH // 2 * BATCH
    in_batches(0, middle, int_of, long_backward)

    @pl.when(me < slices)
    def _():
        def add(i, carry):
            arrive(4, part, parts, i)
            return carry + parts[i]

        total[...] = lax.fori_loop(0, n, add, jnp.zeros((2, TILE), F32))

    in_batches(middle, slices, int_of, long_backward)

    def final_tile(j):
        cols = columns(j)
        far = spread(lag_down, cols, incoming_b[j])
        sums = [jnp.zeros((8, TILE), F32)] * 6
        later = [jnp.zeros((8, TILE), F32)] * 2
        for r in reversed(range(0, rows, CHUNK)):
            part_rows = slice(r, r + CHUNK)
            pgrad = (
                mixed[part_rows, cols] + far[part_rows]
                + skip_ref[0:1, cols] * mgrad[part_rows, cols].astype(F32)
            )
            for which, (other, signal, target) in enumerate(
                ((vmix, k_ref, kmg), (kmix, v_ref, vmg))
            ):
                half = (pgrad * other[part_rows, cols]).astype(BF16)
                target[part_rows, cols] = half
                zero = half.astype(F32)
                wide = jnp.concatenate([zero, later[which]], axis=0)
                shifted = (zero, wide[1 : 1 + CHUNK], wide[2 : 2 + CHUNK])
                later[which] = zero[0:8]
                inside = signal[part_rows, cols].astype(F32)
                for offset in range(3):
                    place = 3 * which + offset
                    sums[place] = sums[place] + folded(shifted[offset] * inside)
        tap_sums = []
        for which in range(2):
            first, second = later[which][0:1], later[which][1:2]
            head_out[2 * which : 2 * which + 2, cols] = later[which][0:2]
            older = tail_in[2 * which : 2 * which + 1, cols]
            newer = tail_in[2 * which + 1 : 2 * which + 2, cols]
            edges = (0.0, first * newer, first * older + second * newer)
            for offset in range(3):
                tap_sums.append(
                    jnp.sum(sums[3 * which + offset], axis=0, keepdims=True) + edges[offset]
                )
        tap_sums = jnp.concatenate(tap_sums + [jnp.zeros((2, TILE), F32)], axis=0)
        high = tap_sums.astype(BF16).astype(F32)
        at = pl.ds(pl.multiple_of(j * 16, 16), 16)
        tap_rows[at, :] = jnp.concatenate([high, tap_sums - high], axis=0).astype(BF16)

    in_batches(
        0, slices, in_turn, final_tile, before=lambda j: arrive(3, suffix, incoming_b, j)
    )

    @pl.when(me > 0)
    def _():
        heads.start()

    @pl.when(me == n - 1)
    def _():
        head_in[...] = jnp.zeros(head_in.shape, F32)

    member = (
        lax.broadcasted_iota(jnp.int32, (TILE, LANES), 0) // group_size
        == lax.broadcasted_iota(jnp.int32, (TILE, LANES), 1)
    ).astype(F32).astype(BF16)
    grouped = jnp.dot(tap_rows[...], member, preferred_element_type=F32)
    fields = [jnp.zeros((8, LANES), F32)] * (mine.shape[1] // LANES)
    for j in range(slices):
        here = grouped[16 * j : 16 * j + 8] + grouped[16 * j + 8 : 16 * j + 16]
        field, start = divmod(j * groups_tile, LANES)
        fields[field] = fields[field] + (pltpu.roll(here, start, 1) if start else here)
    for field, value in enumerate(fields):
        mine[:, field * LANES : (field + 1) * LANES] = value

    @pl.when(me < slices)
    def _():
        mine[6:8, 0:TILE] = total[...]

    @pl.loop(1, n)
    def _(i):
        to_ctx(
            mine, others.at[me], send_sem.at[5], recv_sem.at[5, me], lax.rem(me + i, n)
        ).start()

    def adjoint(j, r):
        cols = columns(j)
        for which, (source, target) in enumerate(((kmg, kg_ref), (vmg, vg_ref))):
            if r + CHUNK < rows:
                wide = source[r : r + CHUNK + 16, cols].astype(F32)
            else:
                wide = jnp.concatenate(
                    [source[r : r + CHUNK, cols].astype(F32), last[which, :, cols]], axis=0
                )
            shifted = (wide[0:CHUNK], wide[1 : 1 + CHUNK], wide[2 : 2 + CHUNK])
            target[r : r + CHUNK, cols] = mix(shifted, cols, 3 * which).astype(BF16)

    def adjoint_upper(j):
        for r in range(0, rows - CHUNK, CHUNK):
            adjoint(j, r)

    in_batches(0, slices, int_of, adjoint_upper)

    @pl.when(me < n - 1)
    def _():
        heads.wait_recv()

    last[0, 0:2] = head_in[0:2]
    last[1, 0:2] = head_in[2:4]

    in_batches(0, slices, int_of, lambda j: adjoint(j, rows - CHUNK))

    others[me] = mine[...]

    def gather(i, carry):
        arrive(5, others, others, i)
        return carry + others[i]

    summed = lax.fori_loop(0, n, gather, jnp.zeros(mine.shape, F32))[:, 0:groups]
    ktg_ref[...] = summed[0:3]
    vtg_ref[...] = summed[3:6]

    def totals_of(j):
        cols = columns(j)
        here = others[j]
        skg_ref[0:1, cols] = here[6:7, 0:TILE]
        gng_ref[0:1, cols] = here[7:8, 0:TILE]

    in_batches(0, slices, int_of, totals_of)

    @pl.when(me < n - 1)
    def _():
        tails.wait_send()

    @pl.when(me > 0)
    def _():
        heads.wait_send()

    for i in range(1, n_ch):
        to_ch(i).wait_send()
    sent_slices(0, own)
    sent_slices(2, own_b)
    sent_slices(4, part)
    sent(5, others, n - 1)

    @pl.when(me < slices)
    def _():
        sent(1, prefix, n - 1)
        sent(3, suffix, n - 1)


def hand_over(count, *refs):
    sources, targets, sems = refs[:count], refs[count : 2 * count], refs[-1]
    stores = [
        pltpu.make_async_copy(sources[i], targets[i], sems.at[i]) for i in range(count)
    ]
    for store in stores:
        store.start()
    for store in stores:
        store.wait()


def local(
    query_proj, key_proj, value_proj, key_taps, value_taps,
    residues, decay_rates, skip_weight, norm_gain, out_grad,
):
    rows, channels = key_proj.shape
    groups, modes = residues.shape
    group_size = channels // groups
    n, n_ch = lax.axis_size("ctx"), lax.axis_size("ch")
    slices = channels // TILE
    assert modes == group_size == 16 and slices <= n and rows == LANES
    field = max(LANES, groups)
    wide_field = max(TILE, field)
    state = lambda count: pltpu.VMEM((count, group_size, TILE), BF16)
    whole = lambda kind: pltpu.VMEM((rows, channels), kind)
    vmem = pl.BlockSpec(memory_space=pltpu.VMEM)
    anywhere = pl.BlockSpec(memory_space=pl.ANY)
    shapes = (
        *([jax.ShapeDtypeStruct((rows, channels), BF16)] * 4),
        *([jax.ShapeDtypeStruct((3, groups), F32)] * 2),
        *([jax.ShapeDtypeStruct((1, channels), F32)] * 2),
    )
    results = pl.pallas_call(
        functools.partial(body, n, n_ch, slices, float(channels * n_ch), group_size),
        out_shape=tuple(pltpu.VMEM(shape.shape, shape.dtype) for shape in shapes),
        in_specs=[anywhere] * 3 + [vmem] * 6 + [anywhere],
        out_specs=(vmem,) * 8,
        scratch_shapes=[
            *([whole(BF16)] * 4), *([pltpu.VMEM((16, channels), BF16)] * 2),
            pltpu.SemaphoreType.DMA((6,)),
            pltpu.VMEM((40, field), F32), pltpu.VMEM((1, channels), F32),
            pltpu.VMEM((4, channels), F32), pltpu.VMEM((4, channels), F32),
            pltpu.VMEM((4, channels), F32), pltpu.VMEM((4, channels), F32),
            pltpu.VMEM((2, 16, channels), F32), pltpu.VMEM((2, 8, channels), F32),
            pltpu.VMEM((8, channels), F32),
            whole(BF16), whole(BF16),
            pltpu.VMEM((channels, rows), BF16), pltpu.VMEM((channels, rows), BF16),
            pltpu.VMEM((groups, rows), F32), pltpu.VMEM((groups, rows), F32),
            pltpu.VMEM((TILE, TILE), BF16),
            whole(BF16), whole(F32), whole(F32), whole(F32), whole(BF16),
            whole(BF16), whole(BF16), pltpu.VMEM((slices * 16, TILE), BF16),
            state(slices), state(n), state(n), state(slices),
            state(slices), state(n), state(n), state(slices),
            pltpu.VMEM((slices, 2, TILE), F32), pltpu.VMEM((n, 2, TILE), F32),
            pltpu.VMEM((2, TILE), F32), pltpu.VMEM((8, wide_field), F32),
            pltpu.VMEM((n, 8, wide_field), F32),
            pltpu.VMEM((2, rows, LANES), F32), pltpu.VMEM((8, 2 * rows), F32),
            pltpu.VMEM((max(1, n_ch - 1), 8, 2 * rows), F32),
            pltpu.SemaphoreType.DMA((2,)), pltpu.SemaphoreType.DMA((2,)),
            pltpu.SemaphoreType.DMA((6,)), pltpu.SemaphoreType.DMA((6, n)),
            pltpu.SemaphoreType.DMA((max(1, n_ch - 1),)), pltpu.SemaphoreType.DMA((max(1, n_ch - 1),)),
        ],
        compiler_params=pltpu.CompilerParams(
            collective_id=0, has_side_effects=True, vmem_limit_bytes=54 << 20
        ),
        name="hyena",
    )(
        query_proj, key_proj, value_proj, key_taps.T, value_taps.T, residues.T, decay_rates.T,
        skip_weight.reshape(1, channels), norm_gain.reshape(1, channels), out_grad,
    )
    results = pl.pallas_call(
        functools.partial(hand_over, len(shapes)),
        out_shape=shapes,
        in_specs=[vmem] * len(shapes),
        out_specs=(anywhere,) * len(shapes),
        scratch_shapes=[pltpu.SemaphoreType.DMA((len(shapes),))],
        compiler_params=pltpu.CompilerParams(vmem_limit_bytes=32 << 20),
        name="hand_over",
    )(*(pltpu.with_memory_space_constraint(result, pltpu.VMEM) for result in results))
    return (
        *results[:4], results[4].T, results[5].T,
        results[6].reshape(channels), results[7].reshape(channels),
    )


def solution(mesh):
    wide = P("ctx", "ch")
    placed = (
        wide, wide, wide, P("ch", None), P("ch", None), P("ch", None), P("ch", None),
        P("ch"), P("ch"), wide,
    )
    return jax.shard_map(
        local, mesh=mesh, in_specs=placed,
        out_specs=(wide, wide, wide, wide, P("ch", None), P("ch", None), P("ch"), P("ch")),
        check_vma=False,
    )
```

```python
import functools

import jax
import jax.numpy as jnp
from jax import lax
from jax.experimental import pallas as pl
from jax.experimental.pallas import tpu as pltpu
from jax.sharding import PartitionSpec as P

EPSILON = 1e-06
TILE = 256
LANES = 128
CHUNK = 32
BATCH = 4
F32, BF16 = jnp.float32, jnp.bfloat16


def halves(wide):
    high = wide.astype(BF16)
    return high, (wide - high.astype(F32)).astype(BF16)


def body(
    n, n_ch, slices, width_all, group_size,
    q_hbm, k_hbm, v_hbm, kt_ref, vt_ref, res_ref, rates_ref, skip_ref, gain_ref, og_hbm,
    out_ref, qg_ref, kg_ref, vg_ref, ktg_ref, vtg_ref, skg_ref, gng_ref,
    q_ref, k_ref, v_ref, og_ref, k_end, v_end, io_sem, small, rate_line,
    tail_out, tail_in, head_out, head_in, before, last, taps,
    lag_up, lag_down, up_turned, down_turned, filt, turned, mask_half,
    prod, kmix, vmix, mixed, mgrad, kmg, vmg, tap_rows,
    own, gathered, prefix, incoming,
    own_b, gathered_b, suffix, incoming_b,
    part, parts, total, mine, others,
    row_acc, row_out, row_in,
    tail_sem, head_sem, send_sem, recv_sem, ch_send, ch_recv,
):
    me = lax.axis_index("ctx")
    me_ch = lax.axis_index("ch")
    rows = q_ref.shape[0]
    groups = rates_ref.shape[1]
    groups_tile = TILE // group_size
    groups_lanes = LANES // group_size
    load_k, load_v, load_q, load_og, load_k_end, load_v_end = (
        pltpu.make_async_copy(src, dst, io_sem.at[place])
        for place, (src, dst) in enumerate((
            (k_hbm, k_ref), (v_hbm, v_ref), (q_hbm, q_ref), (og_hbm, og_ref),
            (k_hbm.at[pl.ds(rows - 16, 16)], k_end), (v_hbm.at[pl.ds(rows - 16, 16)], v_end),
        ))
    )

    def to_ctx(src, dst, s_sem, r_sem, peer):
        return pltpu.make_async_remote_copy(
            src_ref=src, dst_ref=dst, send_sem=s_sem, recv_sem=r_sem,
            device_id={"ctx": peer}, device_id_type=pl.DeviceIdType.MESH,
        )

    def columns(j):
        return pl.ds(pl.multiple_of(j * TILE, TILE), TILE)

    def group_rows(j):
        return pl.ds(pl.multiple_of(j * groups_tile, groups_tile), groups_tile)

    def in_batches(first, last, order, work, before=None, after=None, batch=BATCH):
        batch = batch if first % batch == last % batch == 0 else 1

        @pl.loop(first // batch, last // batch)
        def _(b):
            places = [order(b * batch + u) for u in range(batch)]
            for j in places if before else ():
                before(j)
            for j in places:
                work(j)
            for j in places if after else ():
                after(j)

    def int_of(i):
        return i

    def in_turn(i):
        return lax.rem(me + i, slices)

    def own_last(i):
        return lax.rem(me + BATCH + i, slices)

    barrier = pltpu.get_barrier_semaphore()

    @pl.loop(1, n)
    def _(i):
        pl.semaphore_signal(
            barrier, inc=1, device_id={"ctx": lax.rem(me + i, n)},
            device_id_type=pl.DeviceIdType.MESH,
        )

    for i in range(1, n_ch):
        pl.semaphore_signal(
            barrier, inc=1, device_id={"ch": lax.rem(me_ch + i, n_ch)},
            device_id_type=pl.DeviceIdType.MESH,
        )
    for load in (load_k_end, load_v_end, load_k, load_v, load_q, load_og):
        load.start()

    lane = lax.broadcasted_iota(jnp.int32, (group_size, LANES), 1)
    sub = lax.broadcasted_iota(jnp.int32, (group_size, LANES), 0)
    lane_wide = lane.astype(F32)
    backwards = LANES - 1 - lane
    own_lane = sub == lax.rem(lane, group_size)
    small[...] = jnp.zeros(small.shape, F32)
    small[0:16, 0:groups] = rates_ref[...]
    small[16:32, 0:groups] = res_ref[...]
    small[32:35, 0:groups] = kt_ref[...].astype(F32)
    small[35:38, 0:groups] = vt_ref[...].astype(F32)

    def source_of(first):
        start = (first // LANES) * LANES
        return pl.ds(pl.multiple_of(start, LANES), LANES), first - start

    def pick(table, index):
        return jnp.take_along_axis(table, index, axis=1)

    def of_channels(kind, block):
        source, first = source_of(block * groups_lanes)
        return pick(small[kind, source], first + lane // group_size)

    def lines_of(block):
        cols = pl.ds(pl.multiple_of(block * LANES, LANES), LANES)
        source, first = source_of(block * groups_lanes)
        chosen = first + lane // group_size
        rates = pick(small[0:16, source], chosen)
        rate_line[0:1, cols] = jnp.sum(jnp.where(own_lane, rates, 0.0), axis=0, keepdims=True)
        taps[0:8, cols] = pick(small[32:40, source], chosen[0:8])

    in_batches(0, slices * TILE // LANES, int_of, lines_of)

    block_mask = (
        lax.broadcasted_iota(jnp.int32, (TILE, TILE), 0) // group_size
        == lax.broadcasted_iota(jnp.int32, (TILE, TILE), 1) // group_size
    )
    mask_half[...] = block_mask.astype(F32).astype(BF16)

    row8 = lax.broadcasted_iota(jnp.int32, (8, TILE), 0).astype(F32)
    row_steps = lax.broadcasted_iota(jnp.int32, (rows // 8, TILE), 0).astype(F32) * 8.0

    def of_groups(j):
        source, first = source_of(j * groups_tile)
        for g in range(groups_tile):
            index = jnp.broadcast_to(first + g, (group_size, LANES))
            at = pl.ds(pl.multiple_of(j * TILE + g * group_size, group_size), group_size)
            yield at, pick(small[0:16, source], index), pick(small[16:32, source], index)

    def store_halves(table, at, wide):
        high, low = halves(wide)
        table[at, 0:LANES] = high
        table[at, LANES : 2 * LANES] = low

    def down_turned_of(j):
        for at, rate, _ in of_groups(j):
            store_halves(down_turned, at, jnp.exp(-rate * backwards.astype(F32)))

    def filter_of(j):
        lines = []
        for at, rate, residue in of_groups(j):
            fade = jnp.exp(-rate * lane_wide)
            lines.append(jnp.sum(residue * fade, axis=0, keepdims=True))
            store_halves(up_turned, at, fade)
        lines = jnp.concatenate(lines, axis=0)
        filt[group_rows(j), :] = lines
        turned[group_rows(j), :] = pick(lines, backwards)

    def table_of(table, going_up, j):
        cols = columns(j)
        rate = rate_line[0:1, cols]
        steps = jnp.exp(-rate * row_steps)
        piece = jnp.exp(-rate * (row8 if going_up else 7.0 - row8))
        order = range(rows // 8) if going_up else reversed(range(rows // 8))
        high, low = halves(jnp.concatenate([piece * steps[a : a + 1] for a in order], axis=0))
        table[0:rows, cols] = high
        table[rows : 2 * rows, cols] = low

    in_batches(0, slices, int_of, down_turned_of)

    load_k_end.wait()
    load_v_end.wait()
    tail_out[0:2] = k_end[...].astype(F32)[14:16]
    tail_out[2:4] = v_end[...].astype(F32)[14:16]
    tails = to_ctx(tail_out, tail_in, tail_sem.at[0], tail_sem.at[1], lax.rem(me + 1, n))
    heads = to_ctx(head_out, head_in, head_sem.at[0], head_sem.at[1], lax.rem(me + n - 1, n))
    pl.semaphore_wait(barrier, n - 1 + n_ch - 1)

    @pl.when(me < n - 1)
    def _():
        tails.start()

    @pl.when(me == 0)
    def _():
        tail_in[...] = jnp.zeros(tail_in.shape, F32)

    lane_group = lax.broadcasted_iota(jnp.int32, (CHUNK, TILE), 1) // group_size
    tri_row = lax.broadcasted_iota(jnp.int32, (rows, rows), 0)
    tri_col = lax.broadcasted_iota(jnp.int32, (rows, rows), 1)

    def delayed(ref, cols, which, r):
        if r == 0:
            wide = jnp.concatenate([before[which, :, cols], ref[0:CHUNK, cols].astype(F32)], axis=0)
        else:
            wide = ref[r - 16 : r + CHUNK, cols].astype(F32)
        return wide[16 : 16 + CHUNK], wide[15 : 15 + CHUNK], wide[14 : 14 + CHUNK]

    def mix(parts_of, cols, base):
        zero, one, two = parts_of
        return (
            zero * taps[base : base + 1, cols]
            + one * taps[base + 1 : base + 2, cols]
            + two * taps[base + 2 : base + 3, cols]
        )

    def folded(x):
        return jnp.sum(x.reshape(x.shape[0] // 8, 8, TILE), axis=0)

    def modal(table, j, signal):
        full = jnp.dot(
            table[columns(j), :], jnp.concatenate([signal, signal], axis=0),
            preferred_element_type=F32,
        )
        kept = jnp.where(block_mask, full, 0.0)
        return jnp.sum(kept.reshape(groups_tile, group_size, TILE), axis=0).astype(BF16)

    def spread(table, cols, state):
        big = jnp.concatenate([state] * groups_tile, axis=0) * mask_half[...]
        return jnp.dot(
            jnp.concatenate([table[0:rows, cols], table[rows : 2 * rows, cols]], axis=1),
            jnp.concatenate([big, big], axis=0),
            preferred_element_type=F32,
        )

    def toeplitz(table, shift, j, ref, cols, keep):
        lines = table[group_rows(j), :]
        lhs, rhs = [], []
        for g in range(groups_tile):
            spread_line = jnp.broadcast_to(lines[g : g + 1, :], (rows, rows))
            turned_line = pltpu.roll(spread_line, shift, 1, stride=1, stride_axis=0)
            lhs.append(jnp.where(keep, turned_line, 0.0).astype(BF16))
            for r in range(0, rows, CHUNK):
                wide = ref[r : r + CHUNK, cols].astype(F32)
                rhs.append(jnp.where(lane_group == g, wide, 0.0).astype(BF16))
        return jnp.dot(
            jnp.concatenate(lhs, axis=1), jnp.concatenate(rhs, axis=0),
            preferred_element_type=F32,
        )

    def scatter(phase, source, target, j):
        copy = to_ctx(
            source.at[j], target.at[me], send_sem.at[phase], recv_sem.at[phase, me], j
        )

        @pl.when(j != me)
        def _():
            copy.start()

        @pl.when(j == me)
        def _():
            target[me] = source[j]

    def arrive(phase, source, target, i):
        @pl.when(i != me)
        def _():
            to_ctx(
                source.at[0], target.at[i], send_sem.at[phase], recv_sem.at[phase, i], i
            ).wait_recv()

    def sent(phase, source, count):
        if count:
            whole = source.at[pl.ds(0, count)]
            pltpu.make_async_copy(whole, whole, send_sem.at[phase]).wait()

    def sent_slices(phase, source):
        if n == slices:
            sent(phase, source, slices - 1)
        else:
            @pl.when(me < slices)
            def _():
                sent(phase, source, slices - 1)

            @pl.when(me >= slices)
            def _():
                sent(phase, source, slices)

    def of_owner():
        rate, residue = (
            jnp.concatenate([of_channels(kind, 2 * me), of_channels(kind, 2 * me + 1)], axis=1)
            for kind in (slice(0, 16), slice(16, 32))
        )
        return jnp.exp(-rate * float(rows)), residue * jnp.exp(-rate)

    def mix_rows(cols, r):
        part_rows = slice(r, r + CHUNK)
        key = mix(delayed(k_ref, cols, 0, r), cols, 0)
        value = mix(delayed(v_ref, cols, 1, r), cols, 3)
        kmix[part_rows, cols] = key
        vmix[part_rows, cols] = value
        prod[part_rows, cols] = (key * value).astype(BF16)

    def mix_lower(j):
        for r in range(CHUNK, rows, CHUNK):
            mix_rows(columns(j), r)

    def mix_tile(j):
        mix_rows(columns(j), 0)
        own[j] = modal(down_turned, j, prod[:, columns(j)])

    load_k.wait()
    load_v.wait()
    in_batches(0, slices, int_of, mix_lower)

    @pl.when(me > 0)
    def _():
        tails.wait_recv()

    before[0, 14:16] = tail_in[0:2]
    before[1, 14:16] = tail_in[2:4]
    in_batches(
        0, slices, own_last, mix_tile, after=lambda j: scatter(0, own, gathered, j)
    )

    def long_forward(j):
        cols = columns(j)
        mixed[:, cols] = toeplitz(turned, 1, j, prod, cols, tri_row >= tri_col)

    def scan(taken, own, gathered, given, prefix, incoming, order):
        group = BATCH if n % BATCH == 0 else 1

        @pl.when(me < slices)
        def _():
            fall, scale = of_owner()

            def step(b, carry):
                places = [order(b * group + u) for u in range(group)]
                for place in places:
                    arrive(taken, own, gathered, place)
                for place in places:
                    prefix[place] = (carry * scale).astype(BF16)
                    carry = fall * carry + gathered[place].astype(F32)
                for place in places:
                    scatter(given, prefix, incoming, place)
                return carry

            lax.fori_loop(0, n // group, step, jnp.zeros((group_size, TILE), F32))

    in_batches(0, slices, int_of, filter_of)
    scan(0, own, gathered, 1, prefix, incoming, int_of)
    in_batches(0, slices, int_of, functools.partial(table_of, lag_up, True))
    in_batches(0, slices, int_of, long_forward)

    row_acc[...] = jnp.zeros(row_acc.shape, F32)
    load_q.wait()
    load_og.wait()

    def gate_tile(j):
        cols = columns(j)
        far = spread(lag_up, cols, incoming[j])
        for r in range(0, rows, CHUNK):
            part_rows = slice(r, r + CHUNK)
            full = (
                mixed[part_rows, cols] + far[part_rows]
                + skip_ref[0:1, cols] * prod[part_rows, cols].astype(F32)
            )
            mixed[part_rows, cols] = full
            gated = q_ref[part_rows, cols].astype(F32) * full
            squares = gated * gated
            along = gated * gain_ref[0:1, cols] * og_ref[part_rows, cols].astype(F32)
            row_acc[0, part_rows] += squares[:, :128] + squares[:, 128:]
            row_acc[1, part_rows] += along[:, :128] + along[:, 128:]

    in_batches(
        0, slices, in_turn, gate_tile, before=lambda j: arrive(1, prefix, incoming, j)
    )

    both = row_acc[...].reshape(2 * rows, LANES)
    high, low = halves(both)
    lowest = (both - high.astype(F32) - low.astype(F32)).astype(BF16)
    row_out[...] = lax.dot_general(
        jnp.ones((16, 3 * LANES), BF16), jnp.concatenate([high, low, lowest], axis=1),
        (((1,), (1,)), ((), ())), preferred_element_type=F32,
    )[0:8]

    def to_ch(i):
        return pltpu.make_async_remote_copy(
            src_ref=row_out, dst_ref=row_in.at[i - 1], send_sem=ch_send.at[i - 1],
            recv_sem=ch_recv.at[i - 1], device_id={"ch": lax.rem(me_ch + i, n_ch)},
            device_id_type=pl.DeviceIdType.MESH,
        )

    for i in range(1, n_ch):
        to_ch(i).start()
    in_batches(0, slices, int_of, functools.partial(table_of, lag_down, False))
    summed = row_out[...]
    for i in range(1, n_ch):
        to_ch(i).wait_recv()
        summed = summed + row_in[i - 1]
    squares, along = summed[:, 0:rows], summed[:, rows : 2 * rows]
    scaled = lax.rsqrt(squares / width_all + EPSILON)
    pull = scaled * scaled * scaled * along / width_all
    row_acc[0] = jnp.broadcast_to(scaled[0:1], (rows, rows)).T
    row_acc[1] = jnp.broadcast_to(pull[0:1], (rows, rows)).T

    def gated_parts(part_rows, cols):
        scaled = jnp.concatenate([row_acc[0, part_rows]] * 2, axis=1)
        pull = jnp.concatenate([row_acc[1, part_rows]] * 2, axis=1)
        query = q_ref[part_rows, cols].astype(F32)
        grad = og_ref[part_rows, cols].astype(F32)
        full = mixed[part_rows, cols]
        gated = query * full
        gated_grad = scaled * gain_ref[0:1, cols] * grad - gated * pull
        return scaled, query, grad, full, gated, gated_grad

    def grad_tile(j):
        cols = columns(j)
        for r in range(0, rows, CHUNK):
            part_rows = slice(r, r + CHUNK)
            _, query, _, _, _, gated_grad = gated_parts(part_rows, cols)
            mgrad[part_rows, cols] = (gated_grad * query).astype(BF16)
        own_b[j] = modal(up_turned, j, mgrad[:, cols])

    def output_tile(j):
        cols = columns(j)
        skip_sum = gain_sum = jnp.zeros((8, TILE), F32)
        for r in range(0, rows, CHUNK):
            part_rows = slice(r, r + CHUNK)
            scaled, _, grad, full, gated, gated_grad = gated_parts(part_rows, cols)
            normed = gated * scaled
            out_ref[part_rows, cols] = (normed * gain_ref[0:1, cols]).astype(BF16)
            qg_ref[part_rows, cols] = (gated_grad * full).astype(BF16)
            skip_sum += folded(
                mgrad[part_rows, cols].astype(F32) * prod[part_rows, cols].astype(F32)
            )
            gain_sum += folded(grad * normed)
        part[j, 0:1, :] = jnp.sum(skip_sum, axis=0, keepdims=True)
        part[j, 1:2, :] = jnp.sum(gain_sum, axis=0, keepdims=True)

    in_batches(
        0, slices, own_last, grad_tile, after=lambda j: scatter(2, own_b, gathered_b, j), batch=8
    )
    in_batches(0, slices, own_last, output_tile, after=lambda j: scatter(4, part, parts, j))

    def long_backward(j):
        cols = columns(j)
        mixed[:, cols] = toeplitz(filt, 0, j, mgrad, cols, tri_row <= tri_col)

    scan(2, own_b, gathered_b, 3, suffix, incoming_b, lambda i: n - 1 - i)
    middle = slices // 2 // BATCH * BATCH
    in_batches(0, middle, int_of, long_backward)

    @pl.when(me < slices)
    def _():
        def add(i, carry):
            arrive(4, part, parts, i)
            return carry + parts[i]

        total[...] = lax.fori_loop(0, n, add, jnp.zeros((2, TILE), F32))

    in_batches(middle, slices, int_of, long_backward)

    def final_tile(j):
        cols = columns(j)
        far = spread(lag_down, cols, incoming_b[j])
        sums = [jnp.zeros((8, TILE), F32)] * 6
        later = [jnp.zeros((8, TILE), F32)] * 2
        for r in reversed(range(0, rows, CHUNK)):
            part_rows = slice(r, r + CHUNK)
            pgrad = (
                mixed[part_rows, cols] + far[part_rows]
                + skip_ref[0:1, cols] * mgrad[part_rows, cols].astype(F32)
            )
            for which, (other, signal, target) in enumerate(
                ((vmix, k_ref, kmg), (kmix, v_ref, vmg))
            ):
                half = (pgrad * other[part_rows, cols]).astype(BF16)
                target[part_rows, cols] = half
                zero = half.astype(F32)
                wide = jnp.concatenate([zero, later[which]], axis=0)
                shifted = (zero, wide[1 : 1 + CHUNK], wide[2 : 2 + CHUNK])
                later[which] = zero[0:8]
                inside = signal[part_rows, cols].astype(F32)
                for offset in range(3):
                    place = 3 * which + offset
                    sums[place] = sums[place] + folded(shifted[offset] * inside)
        tap_sums = []
        for which in range(2):
            first, second = later[which][0:1], later[which][1:2]
            head_out[2 * which : 2 * which + 2, cols] = later[which][0:2]
            older = tail_in[2 * which : 2 * which + 1, cols]
            newer = tail_in[2 * which + 1 : 2 * which + 2, cols]
            edges = (0.0, first * newer, first * older + second * newer)
            for offset in range(3):
                tap_sums.append(
                    jnp.sum(sums[3 * which + offset], axis=0, keepdims=True) + edges[offset]
                )
        tap_sums = jnp.concatenate(tap_sums + [jnp.zeros((2, TILE), F32)], axis=0)
        high = tap_sums.astype(BF16).astype(F32)
        at = pl.ds(pl.multiple_of(j * 16, 16), 16)
        tap_rows[at, :] = jnp.concatenate([high, tap_sums - high], axis=0).astype(BF16)

    in_batches(
        0, slices, in_turn, final_tile, before=lambda j: arrive(3, suffix, incoming_b, j)
    )

    @pl.when(me > 0)
    def _():
        heads.start()

    @pl.when(me == n - 1)
    def _():
        head_in[...] = jnp.zeros(head_in.shape, F32)

    member = (
        lax.broadcasted_iota(jnp.int32, (TILE, LANES), 0) // group_size
        == lax.broadcasted_iota(jnp.int32, (TILE, LANES), 1)
    ).astype(F32).astype(BF16)
    grouped = jnp.dot(tap_rows[...], member, preferred_element_type=F32)
    fields = [jnp.zeros((8, LANES), F32)] * (mine.shape[1] // LANES)
    for j in range(slices):
        here = grouped[16 * j : 16 * j + 8] + grouped[16 * j + 8 : 16 * j + 16]
        field, start = divmod(j * groups_tile, LANES)
        fields[field] = fields[field] + (pltpu.roll(here, start, 1) if start else here)
    for field, value in enumerate(fields):
        mine[:, field * LANES : (field + 1) * LANES] = value

    @pl.when(me < slices)
    def _():
        mine[6:8, 0:TILE] = total[...]

    @pl.loop(1, n)
    def _(i):
        to_ctx(
            mine, others.at[me], send_sem.at[5], recv_sem.at[5, me], lax.rem(me + i, n)
        ).start()

    def adjoint(j, r):
        cols = columns(j)
        for which, (source, target) in enumerate(((kmg, kg_ref), (vmg, vg_ref))):
            if r + CHUNK < rows:
                wide = source[r : r + CHUNK + 16, cols].astype(F32)
            else:
                wide = jnp.concatenate(
                    [source[r : r + CHUNK, cols].astype(F32), last[which, :, cols]], axis=0
                )
            shifted = (wide[0:CHUNK], wide[1 : 1 + CHUNK], wide[2 : 2 + CHUNK])
            target[r : r + CHUNK, cols] = mix(shifted, cols, 3 * which).astype(BF16)

    def adjoint_upper(j):
        for r in range(0, rows - CHUNK, CHUNK):
            adjoint(j, r)

    in_batches(0, slices, int_of, adjoint_upper)

    @pl.when(me < n - 1)
    def _():
        heads.wait_recv()

    last[0, 0:2] = head_in[0:2]
    last[1, 0:2] = head_in[2:4]

    in_batches(0, slices, int_of, lambda j: adjoint(j, rows - CHUNK))

    others[me] = mine[...]

    def gather(i, carry):
        arrive(5, others, others, i)
        return carry + others[i]

    summed = lax.fori_loop(0, n, gather, jnp.zeros(mine.shape, F32))[:, 0:groups]
    ktg_ref[...] = summed[0:3]
    vtg_ref[...] = summed[3:6]

    def totals_of(j):
        cols = columns(j)
        here = others[j]
        skg_ref[0:1, cols] = here[6:7, 0:TILE]
        gng_ref[0:1, cols] = here[7:8, 0:TILE]

    in_batches(0, slices, int_of, totals_of)

    @pl.when(me < n - 1)
    def _():
        tails.wait_send()

    @pl.when(me > 0)
    def _():
        heads.wait_send()

    for i in range(1, n_ch):
        to_ch(i).wait_send()
    sent_slices(0, own)
    sent_slices(2, own_b)
    sent_slices(4, part)
    sent(5, others, n - 1)

    @pl.when(me < slices)
    def _():
        sent(1, prefix, n - 1)
        sent(3, suffix, n - 1)


def hand_over(count, *refs):
    sources, targets, sems = refs[:count], refs[count : 2 * count], refs[-1]
    stores = [
        pltpu.make_async_copy(sources[i], targets[i], sems.at[i]) for i in range(count)
    ]
    for store in stores:
        store.start()
    for store in stores:
        store.wait()


def local(
    query_proj, key_proj, value_proj, key_taps, value_taps,
    residues, decay_rates, skip_weight, norm_gain, out_grad,
):
    rows, channels = key_proj.shape
    groups, modes = residues.shape
    group_size = channels // groups
    n, n_ch = lax.axis_size("ctx"), lax.axis_size("ch")
    slices = channels // TILE
    assert modes == group_size == 16 and slices <= n and rows == LANES
    field = max(LANES, groups)
    wide_field = max(TILE, field)
    state = lambda count: pltpu.VMEM((count, group_size, TILE), BF16)
    whole = lambda kind: pltpu.VMEM((rows, channels), kind)
    vmem = pl.BlockSpec(memory_space=pltpu.VMEM)
    anywhere = pl.BlockSpec(memory_space=pl.ANY)
    shapes = (
        *([jax.ShapeDtypeStruct((rows, channels), BF16)] * 4),
        *([jax.ShapeDtypeStruct((3, groups), F32)] * 2),
        *([jax.ShapeDtypeStruct((1, channels), F32)] * 2),
    )
    results = pl.pallas_call(
        functools.partial(body, n, n_ch, slices, float(channels * n_ch), group_size),
        out_shape=tuple(pltpu.VMEM(shape.shape, shape.dtype) for shape in shapes),
        in_specs=[anywhere] * 3 + [vmem] * 6 + [anywhere],
        out_specs=(vmem,) * 8,
        scratch_shapes=[
            *([whole(BF16)] * 4), *([pltpu.VMEM((16, channels), BF16)] * 2),
            pltpu.SemaphoreType.DMA((6,)),
            pltpu.VMEM((40, field), F32), pltpu.VMEM((1, channels), F32),
            pltpu.VMEM((4, channels), F32), pltpu.VMEM((4, channels), F32),
            pltpu.VMEM((4, channels), F32), pltpu.VMEM((4, channels), F32),
            pltpu.VMEM((2, 16, channels), F32), pltpu.VMEM((2, 8, channels), F32),
            pltpu.VMEM((8, channels), F32),
            pltpu.VMEM((2 * rows, channels), BF16), pltpu.VMEM((2 * rows, channels), BF16),
            pltpu.VMEM((channels, 2 * rows), BF16), pltpu.VMEM((channels, 2 * rows), BF16),
            pltpu.VMEM((groups, rows), F32), pltpu.VMEM((groups, rows), F32),
            pltpu.VMEM((TILE, TILE), BF16),
            whole(BF16), whole(F32), whole(F32), whole(F32), whole(BF16),
            whole(BF16), whole(BF16), pltpu.VMEM((slices * 16, TILE), BF16),
            state(slices), state(n), state(n), state(slices),
            state(slices), state(n), state(n), state(slices),
            pltpu.VMEM((slices, 2, TILE), F32), pltpu.VMEM((n, 2, TILE), F32),
            pltpu.VMEM((2, TILE), F32), pltpu.VMEM((8, wide_field), F32),
            pltpu.VMEM((n, 8, wide_field), F32),
            pltpu.VMEM((2, rows, LANES), F32), pltpu.VMEM((8, 2 * rows), F32),
            pltpu.VMEM((max(1, n_ch - 1), 8, 2 * rows), F32),
            pltpu.SemaphoreType.DMA((2,)), pltpu.SemaphoreType.DMA((2,)),
            pltpu.SemaphoreType.DMA((6,)), pltpu.SemaphoreType.DMA((6, n)),
            pltpu.SemaphoreType.DMA((max(1, n_ch - 1),)), pltpu.SemaphoreType.DMA((max(1, n_ch - 1),)),
        ],
        compiler_params=pltpu.CompilerParams(
            collective_id=0, has_side_effects=True, vmem_limit_bytes=54 << 20
        ),
        name="hyena",
    )(
        query_proj, key_proj, value_proj, key_taps.T, value_taps.T, residues.T, decay_rates.T,
        skip_weight.reshape(1, channels), norm_gain.reshape(1, channels), out_grad,
    )
    results = pl.pallas_call(
        functools.partial(hand_over, len(shapes)),
        out_shape=shapes,
        in_specs=[vmem] * len(shapes),
        out_specs=(anywhere,) * len(shapes),
        scratch_shapes=[pltpu.SemaphoreType.DMA((len(shapes),))],
        compiler_params=pltpu.CompilerParams(vmem_limit_bytes=32 << 20),
        name="hand_over",
    )(*(pltpu.with_memory_space_constraint(result, pltpu.VMEM) for result in results))
    return (
        *results[:4], results[4].T, results[5].T,
        results[6].reshape(channels), results[7].reshape(channels),
    )


def solution(mesh):
    wide = P("ctx", "ch")
    placed = (
        wide, wide, wide, P("ch", None), P("ch", None), P("ch", None), P("ch", None),
        P("ch"), P("ch"), wide,
    )
    return jax.shard_map(
        local, mesh=mesh, in_specs=placed,
        out_specs=(wide, wide, wide, wide, P("ch", None), P("ch", None), P("ch"), P("ch")),
        check_vma=False,
    )
```
